128 devices in a mesh: rep: 4 (over y), ep: 32 (over z, x, core).
Axes of the slice: x: 4, y: 4, z: 4, core: 2. Of those that a mesh axis runs over, the one named last changes fastest.
Arguments:
- tokens: bfloat16 [16384, 2048], P(('rep', 'ep')), may hold values from -6 to 6
- expert_ids: int32 [16384, 6], P(('rep', 'ep')), may hold values from 0 to 31, all different within a row; in each aligned block of 128 rows (0 to 127, 128 to 255, ...) at most 32 rows name the same one
- gate_weights: float32 [16384, 6], P(('rep', 'ep')), may hold values from 0.03 to 0.5
- cotangent: bfloat16 [16384, 2048], P(('rep', 'ep')), may hold values from -4 to 4
- w_gate: bfloat16 [32, 2048, 704], P('ep'), may hold values from -0.125 to 0.125
- w_up: bfloat16 [32, 2048, 704], P('ep'), may hold values from -0.125 to 0.125
- w_down: bfloat16 [32, 704, 2048], P('ep'), may hold values from -0.21875 to 0.21875
Outputs:
- mixed: bfloat16 [16384, 2048], P(('rep', 'ep'))
- token_grad: bfloat16 [16384, 2048], P(('rep', 'ep'))
- gate_grad: float32 [16384, 6], P(('rep', 'ep'))
- grad_w_gate: float32 [32, 2048, 704], P('ep', 'rep')
- grad_w_up: float32 [32, 2048, 704], P('ep', 'rep')
- grad_w_down: float32 [32, 704, 2048], P('ep', 'rep')
The draws below stay inside these ranges and needn't reach their ends.
Inputs may be any that keep to these rules, and one draw needn't show every extreme that they name: `expert_ids`: A token's 6 expert ids are distinct; among the tokens of one device no expert is named by more than 32 choices.
All inputs are finite; a program needn't handle non-finite values.
Results may differ from the reference program's by a relative error of at most 0.0085.
Values may be sent and summed in bfloat16 or wider, within the bound.
No kernel may reach another device: no remote copies, remote signals or barrier semaphores. Data moves between devices by JAX's collectives and lax.ppermute only.
A program may use at most 128 MiB of HBM per device.

```python
import math
import jax
import jax.numpy as jnp
import numpy as np
from jax import lax

D = 2048
TOP = 6
FF = 704
TOK_DEV = 128
EXPERTS = 32
CAP = 32
TOKENS = 16384
N_REP = 4
N_EP = 32


def block_scale(key, dims, split, smallest, top_value):
    def one(axis_at, shards_of):
        heights = jax.random.uniform(jax.random.fold_in(jax.random.fold_in(key, 6), axis_at), (shards_of,), jnp.float32, smallest / len(split), top_value / len(split))
        return jnp.repeat(jnp.exp(heights), dims[axis_at] // shards_of).reshape((-1,) + (1,) * (len(dims) - axis_at - 1))

    level = one(*split[0])
    for cut in split[1:]:
        level = level * one(*cut)
    return level


def shared_out(key, own, number, rows, amount, top, limit, lean):
    ranking = jax.random.permutation(key, amount)
    crowded, usual = shares(amount, rows * top, limit, lean, True), shares(amount, rows * top, limit, lean, False)
    places = jnp.arange(amount)

    def named(sizes, offset_by):
        used = int((sizes > 0).sum())
        fixed = max(1, used // 4)
        passed = fixed + (places - fixed + offset_by * (used - fixed)) % max(1, amount - fixed)
        return jnp.zeros((amount,), jnp.int32).at[ranking[jnp.where(places < fixed, places, passed)]].set(jnp.asarray(sizes, jnp.int32))

    sizes = jnp.where(number % 4 == 0, named(crowded, number // 4), named(usual, number - number // 4 - 1))
    mixed = jax.random.permutation(jax.random.fold_in(own, 3), amount)
    giver, receiver = mixed[0:amount // 2 * 2:2], mixed[1:amount // 2 * 2:2]
    margin = jnp.minimum(sizes[giver] - 1, limit - sizes[receiver]) // 2
    margin = jnp.where((giver == ranking[0]) | (receiver == ranking[0]) | (sizes[receiver] == 0), 0, jnp.maximum(margin, 0))
    passed = jax.random.randint(jax.random.fold_in(own, 4), (amount // 2,), 0, 1 << 20) % (margin + 1)
    sizes = sizes.at[giver].add(-passed).at[receiver].add(passed)
    labels = jnp.searchsorted(jnp.cumsum(sizes), jnp.arange(rows * top), side="right").astype(jnp.int32)
    grid = labels.reshape(top, rows).T
    grid = grid[jax.random.permutation(jax.random.fold_in(own, 1), rows)]
    offset_by = jax.random.randint(jax.random.fold_in(own, 2), (rows, 1), 0, top)
    return jnp.take_along_axis(grid, (jnp.arange(top)[None, :] + offset_by) % top, axis=1)


def shares(count, total, limit, skew, full):
    loads = [(1 << 20) // math.isqrt(rank ** skew) + 1 for rank in range(1, count + 1)]
    largest = limit if full else min(limit, max(-(-total // count), total * loads[0] // sum(loads)))
    least = 1 if total - largest >= count - 1 else 0
    given, spare = [largest] + [least] * (count - 1), total - largest - least * (count - 1)
    while spare > 0:
        movable = [i for i in range(1, count) if given[i] < largest] or [i for i in range(1, count) if given[i] < limit]
        whole, remaining = sum([loads[i] for i in movable]), spare
        for i in movable:
            extra = min(limit - given[i], max(1, remaining * loads[i] // whole), spare)
            given[i] = given[i] + extra
            spare = spare - extra
    return np.array(given)


def centred(rng, extent, deviation, most, pieces=(), kind=jnp.bfloat16):
    array = jax.random.normal(rng, extent, jnp.float32) * deviation
    if len(pieces) > 0:
        array = block_scale(rng, extent, pieces, -0.22, 0.18) * array
    return jnp.clip(array, min=-most, max=most).astype(kind)


def setup_inputs(seed: int = 0) -> dict:
    seeds = jax.random.split(jax.random.key(seed), 8)
    tokens = centred(seeds[0], (TOKENS, D), 1.0, 6.0, ((0, 128),))
    expert_ids_keys = jax.random.split(jax.random.fold_in(seeds[1], 1), TOKENS // TOK_DEV)
    expert_ids_turns = jax.random.permutation(jax.random.fold_in(seeds[1], 3), TOKENS // TOK_DEV)
    expert_ids = jax.vmap(lambda own, number: shared_out(jax.random.fold_in(seeds[1], 2), own, number, TOK_DEV, EXPERTS, TOP, CAP, 2))(expert_ids_keys, expert_ids_turns).reshape((TOKENS, TOP))
    gate_weights = jnp.clip(jnp.exp(math.log(0.5) - 2.8134107 * jax.random.uniform(seeds[2], (TOKENS, TOP), jnp.float32) ** block_scale(seeds[2], (TOKENS, TOP), ((0, 128),), -0.2, 0.2)), 0.03, 0.5)
    cotangent = centred(seeds[3], (TOKENS, D), 0.5, 4.0, ((0, 128),))
    w_gate = centred(seeds[4], (EXPERTS, D, FF), D ** -0.5, 0.125, ((0, 32),))
    w_up = centred(seeds[5], (EXPERTS, D, FF), D ** -0.5, 0.125, ((0, 32),))
    w_down = centred(seeds[6], (EXPERTS, FF, D), FF ** -0.5, 0.21875, ((0, 32),))
    return dict(tokens=tokens, expert_ids=expert_ids, gate_weights=gate_weights, cotangent=cotangent, w_gate=w_gate, w_up=w_up, w_down=w_down)


def expert_pass(args):
    rows, d_rows, gate_matrix, up_matrix, down_matrix = args
    gate_pre = jnp.dot(rows, gate_matrix, preferred_element_type=jnp.float32)
    up_pre = jnp.dot(rows, up_matrix, preferred_element_type=jnp.float32)
    sigmoid_val = jax.nn.sigmoid(gate_pre)
    silu_val = gate_pre * sigmoid_val
    act = (silu_val * up_pre).astype(jnp.bfloat16)
    expert_out = jnp.dot(act, down_matrix, preferred_element_type=jnp.float32).astype(jnp.bfloat16)
    act_grad = jnp.dot(d_rows, down_matrix.T, preferred_element_type=jnp.float32)
    gate_pre_grad = (act_grad * up_pre * sigmoid_val * (1.0 + gate_pre * (1.0 - sigmoid_val))).astype(jnp.bfloat16)
    up_pre_grad = (act_grad * silu_val).astype(jnp.bfloat16)
    row_grad = (jnp.dot(gate_pre_grad, gate_matrix.T, preferred_element_type=jnp.float32)
                + jnp.dot(up_pre_grad, up_matrix.T, preferred_element_type=jnp.float32)).astype(jnp.bfloat16)
    part_gate = jnp.dot(rows.T, gate_pre_grad, preferred_element_type=jnp.float32)
    part_up = jnp.dot(rows.T, up_pre_grad, preferred_element_type=jnp.float32)
    part_down = jnp.dot(act.T, d_rows, preferred_element_type=jnp.float32)
    return expert_out, row_grad, part_gate, part_up, part_down


def rounded(value):
    return lax.optimization_barrier(value.astype(jnp.bfloat16)).astype(jnp.float32)


def block_slots(ids_block):
    flat_ids = ids_block.reshape(N_EP, TOK_DEV * TOP)
    onehot = (flat_ids[:, :, None] == jnp.arange(EXPERTS, dtype=jnp.int32)[None, None, :]).astype(jnp.int32)
    before = jnp.cumsum(onehot, axis=1) - onehot
    return jnp.sum(before * onehot, axis=2).reshape(N_EP * TOK_DEV, TOP).astype(jnp.int32)


def reference(tokens, expert_ids, gate_weights, cotangent, w_gate, w_up, w_down):
    group_size = N_EP * TOK_DEV
    pair_count = group_size * TOP
    sum_gate = jnp.zeros((EXPERTS, D, FF), jnp.float32)
    sum_up = jnp.zeros((EXPERTS, D, FF), jnp.float32)
    sum_down = jnp.zeros((EXPERTS, FF, D), jnp.float32)
    mixed_parts = []
    token_parts = []
    gate_parts = []
    for group in range(N_REP):
        low = group * group_size
        high = low + group_size
        tok_block = tokens[low:high]
        ids_block = expert_ids[low:high]
        slot_block = block_slots(ids_block)
        weight_block = gate_weights[low:high]
        cot_block = cotangent[low:high]
        source = (jnp.arange(group_size, dtype=jnp.int32) // TOK_DEV)[:, None]
        slot_index = ((ids_block * N_EP + source) * CAP + slot_block).reshape(-1).astype(jnp.int32)
        slot_owner = jnp.full((EXPERTS * N_EP * CAP,), pair_count, jnp.int32)
        slot_owner = slot_owner.at[slot_index].set(jnp.arange(pair_count, dtype=jnp.int32))
        padded_tokens = jnp.concatenate([tok_block, jnp.zeros((1, D), tok_block.dtype)], axis=0)
        dispatched = padded_tokens[slot_owner // TOP].reshape(EXPERTS, N_EP * CAP, D)
        scaled = (weight_block[:, :, None] * cot_block[:, None, :].astype(jnp.float32)).astype(jnp.bfloat16)
        scaled = jnp.concatenate([scaled.reshape(pair_count, D), jnp.zeros((1, D), scaled.dtype)], axis=0)
        scaled_cot = scaled[slot_owner].reshape(EXPERTS, N_EP * CAP, D)
        outs, row_grads, part_gate, part_up, part_down = lax.map(
            expert_pass, (dispatched, scaled_cot, w_gate, w_up, w_down))
        sum_gate = sum_gate + rounded(part_gate)
        sum_up = sum_up + rounded(part_up)
        sum_down = sum_down + rounded(part_down)
        picked = outs.reshape(-1, D)[slot_index].reshape(group_size, TOP, D).astype(jnp.float32)
        mixed_parts.append(jnp.sum(weight_block[:, :, None] * picked, axis=1).astype(jnp.bfloat16))
        gate_parts.append(jnp.sum(cot_block[:, None, :].astype(jnp.float32) * picked, axis=2))
        back_rows = row_grads.reshape(-1, D)[slot_index].reshape(group_size, TOP, D).astype(jnp.float32)
        token_parts.append(jnp.sum(back_rows, axis=1).astype(jnp.bfloat16))
    mixed = jnp.concatenate(mixed_parts, axis=0)
    token_grad = jnp.concatenate(token_parts, axis=0)
    gate_grad = jnp.concatenate(gate_parts, axis=0)
    return mixed, token_grad, gate_grad, sum_gate, sum_up, sum_down
```

```python
import functools

import jax
import jax.numpy as jnp
from jax import lax
from jax.experimental import pallas as pl
from jax.experimental.pallas import tpu as pltpu
from jax.sharding import PartitionSpec as P


F32 = jnp.float32
BF16 = jnp.bfloat16
SIDE = 4
CORES = 2
LANES = 128
CAP = 32
TOP = 6
DESTS = SIDE * CORES
ROWS = SIDE * CAP


def device_of(z, x, c):
    return (z % SIDE) * SIDE * CORES + (x % SIDE) * CORES + c


def shift_pairs(axis, step, flip):
    pairs = []
    for z in range(SIDE):
        for x in range(SIDE):
            for c in range(CORES):
                there = device_of(z, x + step, c ^ flip) if axis == "x" else device_of(z + step, x, c ^ flip)
                pairs.append((device_of(z, x, c), there))
    return pairs


def move(value, axis, step, flip=0):
    if step % SIDE == 0 and flip == 0:
        return value
    return lax.ppermute(value, "ep", shift_pairs(axis, step, flip))


def position():
    at = lax.axis_index("ep")
    return at >> 3, (at >> 1) & 3, at & 1


def local_experts(axis, offset=0):
    z, x, c = position()
    q = lax.broadcasted_iota(jnp.int32, (DESTS, LANES), 0)
    k, flip = q >> 1, q & 1
    core = (c + flip) & 1
    if axis == "x":
        ids = (z << 3) + (((x + k) & 3) << 1) + core
    else:
        ids = (((z + k) & 3) << 3) + (((x + offset) & 3) << 1) + core
    return ids.astype(F32)


def unpack_meta(part):
    tail = part[LANES : LANES + 8, 0 : 4 * LANES].astype(F32)
    weight = (tail[:, LANES : 2 * LANES] + tail[:, 2 * LANES : 3 * LANES]) + tail[:, 3 * LANES :]
    return tail[:, :LANES], weight


def thirds(value):
    high = value.astype(BF16)
    rest = value - high.astype(F32)
    mid = rest.astype(BF16)
    return high, mid, (rest - mid.astype(F32)).astype(BF16)


def pack_body(tokens, cot, ids, weights, tokens_out, cot_out):
    high, mid, low = thirds(weights[...])
    blank = jnp.zeros((2, LANES), BF16)
    pieces = [jnp.concatenate([p, blank], axis=0) for p in (ids[...].astype(F32).astype(BF16), high, mid, low)]
    width = tokens.shape[1]
    tail = jnp.concatenate(pieces + [jnp.zeros((8, width - 4 * LANES), BF16)], axis=1)
    for source, out in ((tokens, tokens_out), (cot, cot_out)):
        out[0:LANES, :] = source[...]
        out[LANES : LANES + 8, :] = tail


def turn_body(a, b, c, a_out, b_out, c_out):
    a_out[...] = jnp.transpose(a[...])
    b_out[...] = jnp.transpose(b[...])
    c_out[...] = jnp.transpose(c[...])


def selection(part, experts):
    ids, gate = unpack_meta(part)
    named = jnp.zeros((DESTS, LANES), F32)
    weight = jnp.zeros((DESTS, LANES), F32)
    for j in range(TOP):
        hit = ids[j : j + 1, :] == experts
        named = named + jnp.where(hit, 1.0, 0.0)
        weight = weight + jnp.where(hit, gate[j : j + 1, :], 0.0)
    earlier = lax.broadcasted_iota(jnp.int32, (LANES, LANES), 0) < lax.broadcasted_iota(
        jnp.int32, (LANES, LANES), 1
    )
    before = jnp.dot(
        named.astype(BF16), jnp.where(earlier, 1.0, 0.0).astype(BF16), preferred_element_type=F32
    )
    place = jnp.where(named > 0.5, before, -1.0)
    slot = lax.broadcasted_iota(jnp.int32, (CAP, LANES), 0).astype(F32)
    chosen = jnp.concatenate(
        [
            jnp.where(jnp.broadcast_to(place[q : q + 1, :], (CAP, LANES)) == slot, 1.0, 0.0)
            for q in range(DESTS)
        ],
        axis=0,
    )
    spread = jnp.concatenate(
        [jnp.broadcast_to(weight[q : q + 1, :], (CAP, LANES)) for q in range(DESTS)], axis=0
    )
    return chosen, spread


def dispatch_body(axis, scaled, *refs):
    sources, outs = refs[:4], refs[4:]
    experts = local_experts(axis)
    for s in range(SIDE):
        chosen, spread = selection(sources[s], experts)
        rows = jnp.dot(chosen.astype(BF16), sources[s][0:LANES, :], preferred_element_type=F32)
        if scaled:
            rows = rows * jnp.sum(chosen * spread, axis=1, keepdims=True)
        rows = rows.astype(BF16)
        for q in range(DESTS):
            outs[q][s * CAP : (s + 1) * CAP, :] = rows[q * CAP : (q + 1) * CAP, :]


def contract_rows(left, right):
    return lax.dot_general(left, right, (((0,), (0,)), ((), ())), preferred_element_type=F32)


def contract_lanes(left, right):
    return lax.dot_general(left, right, (((1,), (1,)), ((), ())), preferred_element_type=F32)


def combine_out_body(*refs):
    blocks, metas, outs = refs[:8], refs[8:12], refs[12:]
    experts = local_experts("x")
    for s in range(SIDE):
        chosen, spread = selection(metas[s], experts)
        rows = jnp.concatenate([blocks[q][s * CAP : (s + 1) * CAP, :] for q in range(DESTS)], axis=0)
        mix = chosen * spread
        high = mix.astype(BF16)
        low = (mix - high.astype(F32)).astype(BF16)
        outs[s][...] = (contract_rows(high, rows) + contract_rows(low, rows)).astype(BF16)


def combine_grad_body(*refs):
    blocks, metas, outs = refs[:8], refs[8:12], refs[12:]
    experts = local_experts("z")
    columns = []
    for q in range(DESTS):
        product = blocks[q][ROWS : ROWS + 8, 0 : 3 * LANES].astype(F32)
        product = (product[:, :LANES] + product[:, LANES : 2 * LANES]) + product[:, 2 * LANES :]
        columns.append(jnp.transpose(jnp.broadcast_to(product[0:1, :], (LANES, LANES))))
    for s in range(SIDE):
        chosen, _ = selection(metas[s], experts)
        rows = jnp.concatenate([blocks[q][s * CAP : (s + 1) * CAP, :] for q in range(DESTS)], axis=0)
        outs[s][0:LANES, :] = contract_rows(chosen.astype(BF16), rows).astype(BF16)
        gains = jnp.concatenate(
            [
                jnp.sum(
                    chosen[q * CAP : (q + 1) * CAP, :] * columns[q][s * CAP : (s + 1) * CAP, :],
                    axis=0,
                    keepdims=True,
                )
                for q in range(DESTS)
            ],
            axis=0,
        )
        outs[s][LANES : LANES + 8, 0 : 3 * LANES] = jnp.concatenate(thirds(gains), axis=1)
        outs[s][LANES : LANES + 8, 3 * LANES :] = jnp.zeros((8, rows.shape[1] - 3 * LANES), BF16)


def sum_parts_body(*refs):
    parts, out = refs[:4], refs[4]
    out[...] = (
        (parts[0][...].astype(F32) + parts[1][...].astype(F32))
        + (parts[2][...].astype(F32) + parts[3][...].astype(F32))
    ).astype(BF16)


def finish_grad_body(*refs):
    parts, meta, out, gate_out = refs[:4], refs[4], refs[5], refs[6]
    sum_parts_body(*[p.at[0:LANES, :] for p in parts], out)
    ids, gate = unpack_meta(meta)
    total = [jnp.zeros((1, LANES), F32) for _ in range(TOP)]
    for k in range(SIDE):
        experts = local_experts("z", k)
        gains = parts[k][LANES : LANES + 8, 0 : 3 * LANES].astype(F32)
        gains = (gains[:, :LANES] + gains[:, LANES : 2 * LANES]) + gains[:, 2 * LANES :]
        for j in range(TOP):
            hit = ids[j : j + 1, :] == experts
            total[j] = total[j] + jnp.sum(jnp.where(hit, gains, 0.0), axis=0, keepdims=True)
    total = [total[j] / gate[j : j + 1, :] for j in range(TOP)]
    gate_out[...] = jnp.concatenate(total, axis=0)


def forward_body(count, *refs):
    blocks, (gate, up, down) = refs[:count], refs[count : count + 3]
    outs = refs[count + 3 : 2 * count + 3]
    gate_out, up_out, act_out = refs[2 * count + 3 :]
    rows = jnp.concatenate([b[...] for b in blocks], axis=0)
    gate_pre = jnp.dot(rows, gate[...], preferred_element_type=F32)
    up_pre = jnp.dot(rows, up[...], preferred_element_type=F32)
    act = (gate_pre * jax.nn.sigmoid(gate_pre) * up_pre).astype(BF16)
    gate_out[...] = gate_pre
    up_out[...] = up_pre
    act_out[...] = act
    result = jnp.dot(act, down[...], preferred_element_type=F32).astype(BF16)
    for n in range(count):
        outs[n][...] = result[n * ROWS : (n + 1) * ROWS, :]


def hidden_slices(counts):
    place = {}
    for n, ks in enumerate(counts):
        for i, k in enumerate(ks):
            for flip in range(CORES):
                place[2 * k + flip] = (n, (2 * i + flip) * ROWS)
    return place


def backward_body(kzs, place, arrays, *refs):
    count = 2 * len(kzs)
    cots, refs = refs[:count], refs[count:]
    gates, ups, acts, refs = refs[:arrays], refs[arrays : 2 * arrays], refs[2 * arrays : 3 * arrays], refs[3 * arrays :]
    (gate_t, up_t, down_t), refs = refs[:3], refs[3:]
    outs, gate_grad_out, up_grad_out = refs[:count], refs[count], refs[count + 1]

    def ordered(parts):
        pieces = []
        for kz in kzs:
            for flip in range(CORES):
                for kx in range(SIDE):
                    n, first = place[2 * kx + flip]
                    pieces.append(parts[n][first + kz * CAP : first + (kz + 1) * CAP, :])
        return jnp.concatenate(pieces, axis=0)

    cot = jnp.concatenate([c[...] for c in cots], axis=0)
    act_grad = jnp.dot(cot, down_t[...], preferred_element_type=F32)
    gate_pre = ordered(gates)
    up_pre = ordered(ups)
    act = ordered(acts).astype(F32)
    sigmoid_val = jax.nn.sigmoid(gate_pre)
    silu_val = gate_pre * sigmoid_val
    gate_pre_grad = (
        act_grad * up_pre * sigmoid_val * (1.0 + gate_pre * (1.0 - sigmoid_val))
    ).astype(BF16)
    up_pre_grad = (act_grad * silu_val).astype(BF16)
    gate_grad_out[...] = gate_pre_grad
    up_grad_out[...] = up_pre_grad
    product = jnp.sum(act * act_grad, axis=1, keepdims=True)
    result = (
        jnp.dot(gate_pre_grad, gate_t[...], preferred_element_type=F32)
        + jnp.dot(up_pre_grad, up_t[...], preferred_element_type=F32)
    ).astype(BF16)
    width = result.shape[1]
    for n in range(count):
        outs[n][0:ROWS, :] = result[n * ROWS : (n + 1) * ROWS, :]
        part = jnp.broadcast_to(product[n * ROWS : (n + 1) * ROWS, :], (ROWS, LANES))
        part = jnp.transpose(part)[0:8, :]
        outs[n][ROWS : ROWS + 8, 0 : 3 * LANES] = jnp.concatenate(thirds(part), axis=1)
        outs[n][ROWS : ROWS + 8, 3 * LANES :] = jnp.zeros((8, width - 3 * LANES), BF16)


def in_cot_order(blocks, columns, kzs):
    return jnp.concatenate(
        [
            blocks[2 * kx + flip][kz * CAP : (kz + 1) * CAP, columns]
            for kz in kzs
            for flip in range(CORES)
            for kx in range(SIDE)
        ],
        axis=0,
    )


def column_grad_body(order, arrays, *refs):
    gates, ups, blocks, outs = refs[:arrays], refs[arrays : 2 * arrays], refs[2 * arrays : 2 * arrays + 8], refs[2 * arrays + 8 : 2 * arrays + 12]
    turned = refs[2 * arrays + 12]
    rep = lax.axis_index("rep")
    width = outs[0].shape[1]
    hidden = gates[0].shape[1]
    turned[0:hidden, :] = jnp.transpose(jnp.concatenate([h[...] for h in gates], axis=0))
    turned[hidden:, :] = jnp.transpose(jnp.concatenate([h[...] for h in ups], axis=0))
    for k in range(4):
        start = pl.multiple_of(((rep + k) & 3) * width, LANES)
        right = in_cot_order(blocks, pl.ds(start, width), order)
        outs[k][...] = jnp.dot(turned[...], right, preferred_element_type=F32).astype(BF16)


def row_grad_body(place, arrays, *refs):
    acts, blocks, outs = refs[:arrays], refs[arrays : arrays + 8], refs[arrays + 8 : arrays + 12]
    turned, whole = refs[arrays + 12], refs[arrays + 13]
    rep = lax.axis_index("rep")
    height = outs[0].shape[0]
    pieces = []
    for kz in range(SIDE):
        for flip in range(CORES):
            for kx in range(SIDE):
                n, first = place[2 * kx + flip]
                pieces.append(acts[n][first + kz * CAP : first + (kz + 1) * CAP, :])
    turned[...] = jnp.transpose(jnp.concatenate(pieces, axis=0))
    for n in range(4):
        columns = slice(n * 512, (n + 1) * 512)
        right = jnp.concatenate([b[:, columns] for b in blocks], axis=0)
        whole[:, columns] = jnp.dot(turned[...], right, preferred_element_type=F32).astype(BF16)
    for k in range(4):
        start = pl.multiple_of(((rep + k) & 3) * height, 16)
        outs[k][...] = whole[pl.ds(start, height), :]


def call(body, args, outs, flops, scratch=(), name=None):
    moved = sum(a.size * a.dtype.itemsize for a in args) + sum(
        o.size * o.dtype.itemsize for o in outs
    )
    vmem = pl.BlockSpec(memory_space=pltpu.VMEM)
    return pl.pallas_call(
        body,
        out_shape=tuple(outs),
        in_specs=[vmem] * len(args),
        out_specs=tuple([vmem] * len(outs)),
        scratch_shapes=list(scratch),
        cost_estimate=pl.CostEstimate(flops=flops, bytes_accessed=moved, transcendentals=0),
        compiler_params=pltpu.CompilerParams(vmem_limit_bytes=48 * 1024 * 1024),
        name=name,
    )(*args)


def per_device(tokens, expert_ids, gate_weights, cotangent, w_gate, w_up, w_down):
    tok_rows, width = tokens.shape
    gate_t = jnp.swapaxes(w_gate[0], 0, 1)
    up_t = jnp.swapaxes(w_up[0], 0, 1)
    down = w_down[0]
    hidden = down.shape[0]

    def block(dtype=BF16, rows=ROWS, columns=width):
        return jax.ShapeDtypeStruct((rows, columns), dtype)

    tall = block(BF16, ROWS + 8)
    packed_tokens, packed_cot = call(
        pack_body, [tokens, cotangent, expert_ids.T, gate_weights.T], [tall] * 2, 0, name="pack"
    )
    hops = (1, 3, 2)
    token_parts, cot_parts = {0: packed_tokens}, {0: packed_cot}
    for k in hops:
        token_parts[k] = move(packed_tokens, "z", k)
        cot_parts[k] = move(packed_cot, "x", k)
    gate, up, down_t = call(
        turn_body, [gate_t, up_t, down], [block(BF16, width, hidden)] * 3, 0, name="turn"
    )

    def four(parts):
        return [parts[k] for k in range(SIDE)]

    tied = lax.optimization_barrier(four(token_parts) + four(cot_parts))
    from_z, from_x = list(tied[:4]), list(tied[4:])

    gather_flops = 2 * DESTS * ROWS * LANES * width
    sent = call(
        functools.partial(dispatch_body, "x", False), from_z, [block()] * DESTS, gather_flops,
        name="send_rows",
    )
    sent_cot = call(
        functools.partial(dispatch_body, "z", True), from_x, [block()] * DESTS, gather_flops,
        name="send_cot",
    )
    rows = [move(sent[q], "x", q >> 1, q & 1) for q in range(DESTS)]
    cots = [move(sent_cot[q], "z", q >> 1, q & 1) for q in range(DESTS)]

    unit = 2 * ROWS * width * hidden
    groups = ((0,), (1, 3), (2,))
    place = hidden_slices(groups)
    out_blocks, gates, ups, acts = {}, [], [], []
    for ks in groups:
        qs = [2 * k + flip for k in ks for flip in range(CORES)]
        count = len(qs)
        results = call(
            functools.partial(forward_body, count),
            [rows[q] for q in qs] + [gate, up, down],
            [block()] * count + [block(F32, count * ROWS, hidden)] * 2 + [block(BF16, count * ROWS, hidden)],
            3 * count * unit, name="forward",
        )
        for q, value in zip(qs, results):
            out_blocks[q] = value
        gates.append(results[count])
        ups.append(results[count + 1])
        acts.append(results[count + 2])
    out_back = [move(out_blocks[q], "x", -(q >> 1), q & 1) for q in range(DESTS)]

    back_groups = ((1, 3), (2, 0))
    row_blocks, gate_grads, up_grads = {}, [], []
    for ks in back_groups:
        qs = [2 * k + flip for k in ks for flip in range(CORES)]
        count = len(qs)
        results = call(
            functools.partial(backward_body, ks, place, len(groups)),
            [cots[q] for q in qs] + gates + ups + acts + [gate_t, up_t, down_t],
            [tall] * count + [block(BF16, count * ROWS, hidden)] * 2,
            3 * count * unit, name="backward",
        )
        for q, value in zip(qs, results):
            row_blocks[q] = value
        gate_grads.append(results[count])
        up_grads.append(results[count + 1])
    rows_back = [move(row_blocks[q], "z", -(q >> 1), q & 1) for q in range(DESTS)]

    order = tuple(k for ks in back_groups for k in ks)
    down_parts = call(
        functools.partial(row_grad_body, place, len(groups)), acts + cots,
        [block(BF16, hidden // 4, width)] * 4, 8 * unit,
        [pltpu.VMEM((hidden, DESTS * ROWS), BF16), pltpu.VMEM((hidden, width), BF16)],
        name="down_grad",
    )
    both_parts = call(
        functools.partial(column_grad_body, order, len(back_groups)),
        gate_grads + up_grads + rows, [block(BF16, 2 * hidden, width // 4)] * 4, 16 * unit,
        [pltpu.VMEM((2 * hidden, DESTS * ROWS), BF16)], name="gate_up_grad",
    )

    def reduced(parts):
        got = [parts[0]]
        for k in hops:
            got.append(lax.ppermute(parts[k], "rep", [(r, (r + k) % 4) for r in range(4)]))
        got = [g.astype(F32) for g in got]
        return (got[0] + got[1]) + (got[2] + got[3])

    grad_down = reduced(down_parts)[None]
    both = reduced(both_parts)
    grad_gate = jnp.swapaxes(both[:hidden], 0, 1)[None]
    grad_up = jnp.swapaxes(both[hidden:], 0, 1)[None]

    mixed_parts = call(
        combine_out_body, out_back + from_z, [block()] * SIDE, 2 * gather_flops,
        name="combine_out",
    )
    mixed_parts = [move(mixed_parts[s], "z", -s) for s in range(SIDE)]
    (mixed,) = call(sum_parts_body, mixed_parts, [block()], 4 * tok_rows * width, name="mixed")

    grad_parts = call(
        combine_grad_body, rows_back + from_x, [tall] * SIDE, gather_flops, name="combine_grad",
    )
    grad_parts = [move(grad_parts[s], "x", -s) for s in range(SIDE)]
    token_grad, gate_grad = call(
        finish_grad_body, grad_parts + [packed_tokens],
        [block(), block(F32, TOP, LANES)], 4 * tok_rows * width, name="token_grad",
    )
    return (mixed, token_grad, gate_grad.T, grad_gate, grad_up, grad_down)


def solution(mesh):
    placed = (
        P(("rep", "ep"), None),
        P(("rep", "ep"), None),
        P(("rep", "ep"), None),
        P(("rep", "ep"), None),
        P("ep", None, None),
        P("ep", None, None),
        P("ep", None, None),
    )
    return jax.shard_map(
        per_device,
        mesh=mesh,
        in_specs=placed,
        out_specs=(
            P(("rep", "ep"), None),
            P(("rep", "ep"), None),
            P(("rep", "ep"), None),
            P("ep", "rep", None),
            P("ep", "rep", None),
            P("ep", "rep", None),
        ),
        check_vma=False,
    )
```

```python
import functools

import jax
import jax.numpy as jnp
from jax import lax
from jax.experimental import pallas as pl
from jax.experimental.pallas import tpu as pltpu
from jax.sharding import PartitionSpec as P


F32 = jnp.float32
BF16 = jnp.bfloat16
SIDE = 4
CORES = 2
LANES = 128
CAP = 32
TOP = 6
DESTS = SIDE * CORES
ROWS = SIDE * CAP


def device_of(z, x, c):
    return (z % SIDE) * SIDE * CORES + (x % SIDE) * CORES + c


def shift_pairs(axis, step, flip):
    pairs = []
    for z in range(SIDE):
        for x in range(SIDE):
            for c in range(CORES):
                there = device_of(z, x + step, c ^ flip) if axis == "x" else device_of(z + step, x, c ^ flip)
                pairs.append((device_of(z, x, c), there))
    return pairs


def move(value, axis, step, flip=0):
    if step % SIDE == 0 and flip == 0:
        return value
    return lax.ppermute(value, "ep", shift_pairs(axis, step, flip))


def position():
    at = lax.axis_index("ep")
    return at >> 3, (at >> 1) & 3, at & 1


def local_experts(axis, offset=0):
    z, x, c = position()
    q = lax.broadcasted_iota(jnp.int32, (DESTS, LANES), 0)
    k, flip = q >> 1, q & 1
    core = (c + flip) & 1
    if axis == "x":
        ids = (z << 3) + (((x + k) & 3) << 1) + core
    else:
        ids = (((z + k) & 3) << 3) + (((x + offset) & 3) << 1) + core
    return ids.astype(F32)


def unpack_meta(part):
    tail = part[LANES : LANES + 8, 0 : 4 * LANES].astype(F32)
    weight = (tail[:, LANES : 2 * LANES] + tail[:, 2 * LANES : 3 * LANES]) + tail[:, 3 * LANES :]
    return tail[:, :LANES], weight


def thirds(value):
    high = value.astype(BF16)
    rest = value - high.astype(F32)
    mid = rest.astype(BF16)
    return high, mid, (rest - mid.astype(F32)).astype(BF16)


def pack_body(tokens, cot, ids, weights, tokens_out, cot_out):
    high, mid, low = thirds(weights[...])
    blank = jnp.zeros((2, LANES), BF16)
    pieces = [jnp.concatenate([p, blank], axis=0) for p in (ids[...].astype(F32).astype(BF16), high, mid, low)]
    width = tokens.shape[1]
    tail = jnp.concatenate(pieces + [jnp.zeros((8, width - 4 * LANES), BF16)], axis=1)
    for source, out in ((tokens, tokens_out), (cot, cot_out)):
        out[0:LANES, :] = source[...]
        out[LANES : LANES + 8, :] = tail


def turn_body(a, b, c, a_out, b_out, c_out):
    a_out[...] = jnp.transpose(a[...])
    b_out[...] = jnp.transpose(b[...])
    c_out[...] = jnp.transpose(c[...])


def selection(part, experts):
    ids, gate = unpack_meta(part)
    named = jnp.zeros((DESTS, LANES), F32)
    weight = jnp.zeros((DESTS, LANES), F32)
    for j in range(TOP):
        hit = ids[j : j + 1, :] == experts
        named = named + jnp.where(hit, 1.0, 0.0)
        weight = weight + jnp.where(hit, gate[j : j + 1, :], 0.0)
    earlier = lax.broadcasted_iota(jnp.int32, (LANES, LANES), 0) < lax.broadcasted_iota(
        jnp.int32, (LANES, LANES), 1
    )
    before = jnp.dot(
        named.astype(BF16), jnp.where(earlier, 1.0, 0.0).astype(BF16), preferred_element_type=F32
    )
    place = jnp.where(named > 0.5, before, -1.0)
    slot = lax.broadcasted_iota(jnp.int32, (CAP, LANES), 0).astype(F32)
    chosen = jnp.concatenate(
        [
            jnp.where(jnp.broadcast_to(place[q : q + 1, :], (CAP, LANES)) == slot, 1.0, 0.0)
            for q in range(DESTS)
        ],
        axis=0,
    )
    spread = jnp.concatenate(
        [jnp.broadcast_to(weight[q : q + 1, :], (CAP, LANES)) for q in range(DESTS)], axis=0
    )
    return chosen, spread


def dispatch_body(axis, scaled, *refs):
    sources, outs = refs[:4], refs[4:]
    experts = local_experts(axis)
    for s in range(SIDE):
        chosen, spread = selection(sources[s], experts)
        rows = jnp.dot(chosen.astype(BF16), sources[s][0:LANES, :], preferred_element_type=F32)
        if scaled:
            rows = rows * jnp.sum(chosen * spread, axis=1, keepdims=True)
        rows = rows.astype(BF16)
        for q in range(DESTS):
            outs[q][s * CAP : (s + 1) * CAP, :] = rows[q * CAP : (q + 1) * CAP, :]


def contract_rows(left, right):
    return lax.dot_general(left, right, (((0,), (0,)), ((), ())), preferred_element_type=F32)


def combine_out_body(*refs):
    blocks, metas, outs = refs[:8], refs[8:12], refs[12:]
    experts = local_experts("x")
    for s in range(SIDE):
        chosen, spread = selection(metas[s], experts)
        rows = jnp.concatenate([blocks[q][s * CAP : (s + 1) * CAP, :] for q in range(DESTS)], axis=0)
        mix = chosen * spread
        high = mix.astype(BF16)
        low = (mix - high.astype(F32)).astype(BF16)
        outs[s][...] = (contract_rows(high, rows) + contract_rows(low, rows)).astype(BF16)


def combine_grad_body(*refs):
    blocks, metas, outs = refs[:8], refs[8:12], refs[12:]
    experts = local_experts("z")
    columns = []
    for q in range(DESTS):
        product = blocks[q][ROWS : ROWS + 8, 0 : 3 * LANES].astype(F32)
        product = (product[:, :LANES] + product[:, LANES : 2 * LANES]) + product[:, 2 * LANES :]
        columns.append(jnp.transpose(jnp.broadcast_to(product[0:1, :], (LANES, LANES))))
    for s in range(SIDE):
        chosen, _ = selection(metas[s], experts)
        rows = jnp.concatenate([blocks[q][s * CAP : (s + 1) * CAP, :] for q in range(DESTS)], axis=0)
        outs[s][0:LANES, :] = contract_rows(chosen.astype(BF16), rows).astype(BF16)
        gains = jnp.concatenate(
            [
                jnp.sum(
                    chosen[q * CAP : (q + 1) * CAP, :] * columns[q][s * CAP : (s + 1) * CAP, :],
                    axis=0,
                    keepdims=True,
                )
                for q in range(DESTS)
            ],
            axis=0,
        )
        outs[s][LANES : LANES + 8, 0 : 3 * LANES] = jnp.concatenate(thirds(gains), axis=1)
        outs[s][LANES : LANES + 8, 3 * LANES :] = jnp.zeros((8, rows.shape[1] - 3 * LANES), BF16)


def sum_parts_body(*refs):
    parts, out = refs[:4], refs[4]
    out[...] = (
        (parts[0][...].astype(F32) + parts[1][...].astype(F32))
        + (parts[2][...].astype(F32) + parts[3][...].astype(F32))
    ).astype(BF16)


def finish_grad_body(*refs):
    parts, meta, out, gate_out = refs[:4], refs[4], refs[5], refs[6]
    sum_parts_body(*[p.at[0:LANES, :] for p in parts], out)
    ids, gate = unpack_meta(meta)
    total = [jnp.zeros((1, LANES), F32) for _ in range(TOP)]
    for k in range(SIDE):
        experts = local_experts("z", k)
        gains = parts[k][LANES : LANES + 8, 0 : 3 * LANES].astype(F32)
        gains = (gains[:, :LANES] + gains[:, LANES : 2 * LANES]) + gains[:, 2 * LANES :]
        for j in range(TOP):
            hit = ids[j : j + 1, :] == experts
            total[j] = total[j] + jnp.sum(jnp.where(hit, gains, 0.0), axis=0, keepdims=True)
    total = [total[j] / gate[j : j + 1, :] for j in range(TOP)]
    gate_out[...] = jnp.concatenate(total, axis=0)


def forward_body(count, *refs):
    blocks, (gate, up, down) = refs[:count], refs[count : count + 3]
    outs = refs[count + 3 : 2 * count + 3]
    gate_out, up_out, act_out = refs[2 * count + 3 :]
    rows = jnp.concatenate([b[...] for b in blocks], axis=0)
    gate_pre = jnp.dot(rows, gate[...], preferred_element_type=F32)
    up_pre = jnp.dot(rows, up[...], preferred_element_type=F32)
    act = (gate_pre * jax.nn.sigmoid(gate_pre) * up_pre).astype(BF16)
    gate_out[...] = gate_pre
    up_out[...] = up_pre
    act_out[...] = act
    result = jnp.dot(act, down[...], preferred_element_type=F32).astype(BF16)
    for n in range(count):
        outs[n][...] = result[n * ROWS : (n + 1) * ROWS, :]


def hidden_slices(counts):
    place = {}
    for n, ks in enumerate(counts):
        for i, k in enumerate(ks):
            for flip in range(CORES):
                place[2 * k + flip] = (n, (2 * i + flip) * ROWS)
    return place


def backward_body(kzs, place, arrays, *refs):
    count = 2 * len(kzs)
    cots, refs = refs[:count], refs[count:]
    gates, ups, acts, refs = refs[:arrays], refs[arrays : 2 * arrays], refs[2 * arrays : 3 * arrays], refs[3 * arrays :]
    (gate_t, up_t, down_t), refs = refs[:3], refs[3:]
    outs, gate_grad_out, up_grad_out = refs[:count], refs[count], refs[count + 1]

    def ordered(parts):
        pieces = []
        for kz in kzs:
            for flip in range(CORES):
                for kx in range(SIDE):
                    n, first = place[2 * kx + flip]
                    pieces.append(parts[n][first + kz * CAP : first + (kz + 1) * CAP, :])
        return jnp.concatenate(pieces, axis=0)

    cot = jnp.concatenate([c[...] for c in cots], axis=0)
    act_grad = jnp.dot(cot, down_t[...], preferred_element_type=F32)
    gate_pre = ordered(gates)
    up_pre = ordered(ups)
    act = ordered(acts).astype(F32)
    sigmoid_val = jax.nn.sigmoid(gate_pre)
    silu_val = gate_pre * sigmoid_val
    gate_pre_grad = (
        act_grad * up_pre * sigmoid_val * (1.0 + gate_pre * (1.0 - sigmoid_val))
    ).astype(BF16)
    up_pre_grad = (act_grad * silu_val).astype(BF16)
    gate_grad_out[...] = gate_pre_grad
    up_grad_out[...] = up_pre_grad
    product = jnp.sum(act * act_grad, axis=1, keepdims=True)
    result = (
        jnp.dot(gate_pre_grad, gate_t[...], preferred_element_type=F32)
        + jnp.dot(up_pre_grad, up_t[...], preferred_element_type=F32)
    ).astype(BF16)
    width = result.shape[1]
    for n in range(count):
        outs[n][0:ROWS, :] = result[n * ROWS : (n + 1) * ROWS, :]
        part = jnp.broadcast_to(product[n * ROWS : (n + 1) * ROWS, :], (ROWS, LANES))
        part = jnp.transpose(part)[0:8, :]
        outs[n][ROWS : ROWS + 8, 0 : 3 * LANES] = jnp.concatenate(thirds(part), axis=1)
        outs[n][ROWS : ROWS + 8, 3 * LANES :] = jnp.zeros((8, width - 3 * LANES), BF16)


def in_cot_order(blocks, columns, kzs):
    return jnp.concatenate(
        [
            blocks[2 * kx + flip][kz * CAP : (kz + 1) * CAP, columns]
            for kz in kzs
            for flip in range(CORES)
            for kx in range(SIDE)
        ],
        axis=0,
    )


def column_grad_body(order, arrays, *refs):
    gates, ups, blocks, outs = refs[:arrays], refs[arrays : 2 * arrays], refs[2 * arrays : 2 * arrays + 8], refs[2 * arrays + 8 : 2 * arrays + 12]
    turned = refs[2 * arrays + 12]
    rep = lax.axis_index("rep")
    width = outs[0].shape[1]
    hidden = gates[0].shape[1]
    turned[0:hidden, :] = jnp.transpose(jnp.concatenate([h[...] for h in gates], axis=0))
    turned[hidden:, :] = jnp.transpose(jnp.concatenate([h[...] for h in ups], axis=0))
    for k in range(4):
        start = pl.multiple_of(((rep + k) & 3) * width, LANES)
        right = in_cot_order(blocks, pl.ds(start, width), order)
        outs[k][...] = jnp.dot(turned[...], right, preferred_element_type=F32).astype(BF16)


def row_grad_body(place, arrays, *refs):
    acts, blocks, outs = refs[:arrays], refs[arrays : arrays + 8], refs[arrays + 8 : arrays + 12]
    turned, whole = refs[arrays + 12], refs[arrays + 13]
    rep = lax.axis_index("rep")
    height = outs[0].shape[0]
    pieces = []
    for kz in range(SIDE):
        for flip in range(CORES):
            for kx in range(SIDE):
                n, first = place[2 * kx + flip]
                pieces.append(acts[n][first + kz * CAP : first + (kz + 1) * CAP, :])
    turned[...] = jnp.transpose(jnp.concatenate(pieces, axis=0))
    for n in range(4):
        columns = slice(n * 512, (n + 1) * 512)
        right = jnp.concatenate([b[:, columns] for b in blocks], axis=0)
        whole[:, columns] = jnp.dot(turned[...], right, preferred_element_type=F32).astype(BF16)
    for k in range(4):
        start = pl.multiple_of(((rep + k) & 3) * height, 16)
        outs[k][...] = whole[pl.ds(start, height), :]


def call(body, args, outs, flops, scratch=(), limit=32):
    moved = sum(a.size * a.dtype.itemsize for a in args) + sum(
        o.size * o.dtype.itemsize for o in outs
    )
    vmem = pl.BlockSpec(memory_space=pltpu.VMEM)
    return pl.pallas_call(
        body,
        out_shape=tuple(outs),
        in_specs=[vmem] * len(args),
        out_specs=tuple([vmem] * len(outs)),
        scratch_shapes=list(scratch),
        cost_estimate=pl.CostEstimate(flops=flops, bytes_accessed=moved, transcendentals=0),
        compiler_params=pltpu.CompilerParams(vmem_limit_bytes=limit * 1024 * 1024),
    )(*args)


def per_device(tokens, expert_ids, gate_weights, cotangent, w_gate, w_up, w_down):
    tok_rows, width = tokens.shape
    gate_t = jnp.swapaxes(w_gate[0], 0, 1)
    up_t = jnp.swapaxes(w_up[0], 0, 1)
    down = w_down[0]
    hidden = down.shape[0]

    def block(dtype=BF16, rows=ROWS, columns=width):
        return jax.ShapeDtypeStruct((rows, columns), dtype)

    tall = block(BF16, ROWS + 8)
    packed_tokens, packed_cot = call(
        pack_body, [tokens, cotangent, expert_ids.T, gate_weights.T], [tall] * 2, 0, limit=8
    )
    hops = (1, 3, 2)
    token_parts, cot_parts = {0: packed_tokens}, {0: packed_cot}
    for k in hops:
        token_parts[k] = move(packed_tokens, "z", k, 0)
        cot_parts[k] = move(packed_cot, "x", k, 0)
    gate, up, down_t = call(turn_body, [gate_t, up_t, down], [block(BF16, width, hidden)] * 3, 0, limit=20)

    def four(parts):
        return [parts[k] for k in range(SIDE)]

    tied = lax.optimization_barrier(four(token_parts) + four(cot_parts))
    from_z, from_x = list(tied[:4]), list(tied[4:])

    gather_flops = 2 * DESTS * ROWS * LANES * width
    sent = call(
        functools.partial(dispatch_body, "x", False), from_z, [block()] * DESTS, gather_flops,
        limit=16,
    )
    sent_cot = call(
        functools.partial(dispatch_body, "z", True), from_x, [block()] * DESTS, gather_flops,
        limit=16,
    )
    rows = [move(sent[q], "x", q >> 1, q & 1) for q in range(DESTS)]
    cots = [move(sent_cot[q], "z", q >> 1, q & 1) for q in range(DESTS)]

    unit = 2 * ROWS * width * hidden
    groups = ((0,), (1, 3), (2,))
    place = hidden_slices(groups)
    out_blocks, gates, ups, acts = {}, [], [], []
    for ks in groups:
        qs = [2 * k + flip for k in ks for flip in range(CORES)]
        count = len(qs)
        results = call(
            functools.partial(forward_body, count),
            [rows[q] for q in qs] + [gate, up, down],
            [block()] * count + [block(F32, count * ROWS, hidden)] * 2 + [block(BF16, count * ROWS, hidden)],
            3 * count * unit, limit=28,
        )
        for q, value in zip(qs, results):
            out_blocks[q] = value
        gates.append(results[count])
        ups.append(results[count + 1])
        acts.append(results[count + 2])
    out_back = [move(out_blocks[q], "x", -(q >> 1), q & 1) for q in range(DESTS)]

    back_groups = ((1, 3), (2, 0))
    row_blocks, gate_grads, up_grads = {}, [], []
    for ks in back_groups:
        qs = [2 * k + flip for k in ks for flip in range(CORES)]
        count = len(qs)
        results = call(
            functools.partial(backward_body, ks, place, len(groups)),
            [cots[q] for q in qs] + gates + ups + acts + [gate_t, up_t, down_t],
            [tall] * count + [block(BF16, count * ROWS, hidden)] * 2,
            3 * count * unit, limit=32,
        )
        for q, value in zip(qs, results):
            row_blocks[q] = value
        gate_grads.append(results[count])
        up_grads.append(results[count + 1])
    rows_back = [move(row_blocks[q], "z", -(q >> 1), q & 1) for q in range(DESTS)]

    order = tuple(k for ks in back_groups for k in ks)
    down_parts = call(
        functools.partial(row_grad_body, place, len(groups)), acts + cots,
        [block(BF16, hidden // 4, width)] * 4, 8 * unit,
        [pltpu.VMEM((hidden, DESTS * ROWS), BF16), pltpu.VMEM((hidden, width), BF16)],
    )
    both_parts = call(
        functools.partial(column_grad_body, order, len(back_groups)),
        gate_grads + up_grads + rows, [block(BF16, 2 * hidden, width // 4)] * 4, 16 * unit,
        [pltpu.VMEM((2 * hidden, DESTS * ROWS), BF16)],
    )

    def reduced(parts):
        got = [parts[0]]
        for k in hops:
            got.append(lax.ppermute(parts[k], "rep", [(r, (r + k) % 4) for r in range(4)]))
        got = [g.astype(F32) for g in got]
        return (got[0] + got[1]) + (got[2] + got[3])

    grad_down = reduced(down_parts)[None]
    both = reduced(both_parts)
    grad_gate = jnp.swapaxes(both[:hidden], 0, 1)[None]
    grad_up = jnp.swapaxes(both[hidden:], 0, 1)[None]

    mixed_parts = call(
        combine_out_body, out_back + from_z, [block()] * SIDE, 2 * gather_flops,
        limit=16,
    )
    mixed_parts = [move(mixed_parts[s], "z", -s, 0) for s in range(SIDE)]
    (mixed,) = call(sum_parts_body, mixed_parts, [block()], 4 * tok_rows * width, limit=8)

    grad_parts = call(combine_grad_body, rows_back + from_x, [tall] * SIDE, gather_flops, limit=16)
    grad_parts = [move(grad_parts[s], "x", -s, 0) for s in range(SIDE)]
    token_grad, gate_grad = call(
        finish_grad_body, grad_parts + [packed_tokens],
        [block(), block(F32, TOP, LANES)], 4 * tok_rows * width, limit=8,
    )
    return (mixed, token_grad, gate_grad.T, grad_gate, grad_up, grad_down)


def solution(mesh):
    placed = (
        P(("rep", "ep"), None),
        P(("rep", "ep"), None),
        P(("rep", "ep"), None),
        P(("rep", "ep"), None),
        P("ep", None, None),
        P("ep", None, None),
        P("ep", None, None),
    )

    return jax.shard_map(
        per_device,
        mesh=mesh,
        in_specs=placed,
        out_specs=(
            P(("rep", "ep"), None),
            P(("rep", "ep"), None),
            P(("rep", "ep"), None),
            P("ep", "rep", None),
            P("ep", "rep", None),
            P("ep", "rep", None),
        ),
        check_vma=False,
    )
```

```python
import functools

import jax
import jax.numpy as jnp
from jax import lax
from jax.experimental import pallas as pl
from jax.experimental.pallas import tpu as pltpu
from jax.sharding import PartitionSpec as P


F32 = jnp.float32
BF16 = jnp.bfloat16
SIDE = 4
CORES = 2
LANES = 128
CAP = 32
TOP = 6
DESTS = SIDE * CORES
TILE = 512
ROWS = SIDE * CAP


def device_of(z, x, c):
    return (z % SIDE) * SIDE * CORES + (x % SIDE) * CORES + c


def shift_pairs(axis, step, flip):
    pairs = []
    for z in range(SIDE):
        for x in range(SIDE):
            for c in range(CORES):
                there = device_of(z, x + step, c ^ flip) if axis == "x" else device_of(z + step, x, c ^ flip)
                pairs.append((device_of(z, x, c), there))
    return pairs


def move(value, axis, step, flip=0):
    if step % SIDE == 0 and flip == 0:
        return value
    return lax.ppermute(value, "ep", shift_pairs(axis, step, flip))


def position():
    at = lax.axis_index("ep")
    return at >> 3, (at >> 1) & 3, at & 1


def local_experts(axis, offset=0):
    z, x, c = position()
    q = lax.broadcasted_iota(jnp.int32, (DESTS, LANES), 0)
    k, flip = q >> 1, q & 1
    core = (c + flip) & 1
    if axis == "x":
        ids = (z << 3) + (((x + k) & 3) << 1) + core
    else:
        ids = (((z + k) & 3) << 3) + (((x + offset) & 3) << 1) + core
    return ids.astype(F32)


def unpack_meta(part):
    tail = part[LANES : LANES + 8, 0 : 4 * LANES].astype(F32)
    weight = (tail[:, LANES : 2 * LANES] + tail[:, 2 * LANES : 3 * LANES]) + tail[:, 3 * LANES :]
    return tail[:, :LANES], weight


def thirds(value):
    high = value.astype(BF16)
    rest = value - high.astype(F32)
    mid = rest.astype(BF16)
    return high, mid, (rest - mid.astype(F32)).astype(BF16)


def pack_body(tokens, cot, ids, weights, tokens_out, cot_out, ids_here, weights_here, done):
    copies = [
        pltpu.make_async_copy(source, there, done.at[n])
        for n, (source, there) in enumerate((
            (ids, ids_here), (weights, weights_here),
            (tokens, tokens_out.at[0:LANES, :]), (cot, cot_out.at[0:LANES, :]),
        ))
    ]
    for copy in copies:
        copy.start()
    for copy in copies[:2]:
        copy.wait()
    high, mid, low = thirds(weights_here[...])
    blank = jnp.zeros((2, LANES), BF16)
    names = ids_here[...].astype(F32).astype(BF16)
    pieces = [jnp.concatenate([p, blank], axis=0) for p in (names, high, mid, low)]
    width = tokens.shape[1]
    tail = jnp.concatenate(pieces + [jnp.zeros((8, width - 4 * LANES), BF16)], axis=1)
    for out in (tokens_out, cot_out):
        out[LANES : LANES + 8, :] = tail
    for copy in copies[2:]:
        copy.wait()


def selection(part, experts):
    ids, gate = unpack_meta(part)
    named = jnp.zeros((DESTS, LANES), F32)
    weight = jnp.zeros((DESTS, LANES), F32)
    for j in range(TOP):
        hit = ids[j : j + 1, :] == experts
        named = named + jnp.where(hit, 1.0, 0.0)
        weight = weight + jnp.where(hit, gate[j : j + 1, :], 0.0)
    earlier = lax.broadcasted_iota(jnp.int32, (LANES, LANES), 0) < lax.broadcasted_iota(
        jnp.int32, (LANES, LANES), 1
    )
    before = jnp.dot(
        named.astype(BF16), jnp.where(earlier, 1.0, 0.0).astype(BF16), preferred_element_type=F32
    )
    place = jnp.where(named > 0.5, before, -1.0)
    slot = lax.broadcasted_iota(jnp.int32, (CAP, LANES), 0).astype(F32)
    chosen = jnp.concatenate(
        [
            jnp.where(jnp.broadcast_to(place[q : q + 1, :], (CAP, LANES)) == slot, 1.0, 0.0)
            for q in range(DESTS)
        ],
        axis=0,
    )
    spread = jnp.concatenate(
        [jnp.broadcast_to(weight[q : q + 1, :], (CAP, LANES)) for q in range(DESTS)], axis=0
    )
    return chosen, spread


def dispatch_body(axis, scaled, *refs):
    sources, outs = refs[:4], refs[4:]
    experts = local_experts(axis)
    for s in range(SIDE):
        chosen, spread = selection(sources[s], experts)
        scale = jnp.sum(chosen * spread, axis=1, keepdims=True) if scaled else None
        chosen = chosen.astype(BF16)

        def column(n, carry, s=s, chosen=chosen, scale=scale):
            at = pl.ds(pl.multiple_of(n * TILE, TILE), TILE)
            rows = jnp.dot(chosen, sources[s][0:LANES, at], preferred_element_type=F32)
            if scaled:
                rows = rows * scale
            rows = rows.astype(BF16)
            for q in range(DESTS):
                outs[q][s * CAP : (s + 1) * CAP, at] = rows[q * CAP : (q + 1) * CAP, :]
            return carry

        lax.fori_loop(0, outs[0].shape[1] // TILE, column, 0)


def contract_rows(left, right):
    return lax.dot_general(left, right, (((0,), (0,)), ((), ())), preferred_element_type=F32)


def contract_lanes(left, right):
    return lax.dot_general(left, right, (((1,), (1,)), ((), ())), preferred_element_type=F32)


def source_rows(blocks, s, columns):
    return jnp.concatenate(
        [blocks[q][s * CAP : (s + 1) * CAP, columns] for q in range(DESTS)], axis=0
    )


def combine_out_body(*refs):
    blocks, metas, outs = refs[:8], refs[8:12], refs[12:]
    experts = local_experts("x")
    for s in range(SIDE):
        chosen, spread = selection(metas[s], experts)
        mix = chosen * spread
        high = mix.astype(BF16)
        mix = jnp.concatenate([high, (mix - high.astype(F32)).astype(BF16)], axis=1)

        def column(n, carry, s=s, mix=mix):
            at = pl.ds(pl.multiple_of(n * TILE, TILE), TILE)
            both = contract_rows(mix, source_rows(blocks, s, at))
            outs[s][:, at] = (both[:LANES, :] + both[LANES:, :]).astype(BF16)
            return carry

        lax.fori_loop(0, outs[0].shape[1] // TILE, column, 0)


def combine_grad_body(*refs):
    blocks, metas, outs = refs[:8], refs[8:12], refs[12:]
    experts = local_experts("z")
    columns = []
    for q in range(DESTS):
        product = blocks[q][ROWS : ROWS + 8, 0 : 3 * LANES].astype(F32)
        product = (product[:, :LANES] + product[:, LANES : 2 * LANES]) + product[:, 2 * LANES :]
        columns.append(jnp.transpose(jnp.broadcast_to(product[0:1, :], (LANES, LANES))))
    for s in range(SIDE):
        chosen, _ = selection(metas[s], experts)
        picked = chosen.astype(BF16)

        def column(n, carry, s=s, picked=picked):
            at = pl.ds(pl.multiple_of(n * TILE, TILE), TILE)
            outs[s][0:LANES, at] = contract_rows(picked, source_rows(blocks, s, at)).astype(BF16)
            return carry

        width = outs[0].shape[1]
        lax.fori_loop(0, width // TILE, column, 0)
        gains = jnp.concatenate(
            [
                jnp.sum(
                    chosen[q * CAP : (q + 1) * CAP, :] * columns[q][s * CAP : (s + 1) * CAP, :],
                    axis=0,
                    keepdims=True,
                )
                for q in range(DESTS)
            ],
            axis=0,
        )
        outs[s][LANES : LANES + 8, 0 : 3 * LANES] = jnp.concatenate(thirds(gains), axis=1)
        outs[s][LANES : LANES + 8, 3 * LANES :] = jnp.zeros((8, width - 3 * LANES), BF16)


def sum_parts_body(*refs):
    parts, out = refs[:4], refs[4]
    out[...] = (
        (parts[0][...].astype(F32) + parts[1][...].astype(F32))
        + (parts[2][...].astype(F32) + parts[3][...].astype(F32))
    ).astype(BF16)


def finish_grad_body(*refs):
    parts, meta, out, gate_out = refs[:4], refs[4], refs[5], refs[6]
    sum_parts_body(*[p.at[0:LANES, :] for p in parts], out)
    ids, gate = unpack_meta(meta)
    total = [jnp.zeros((1, LANES), F32) for _ in range(TOP)]
    for k in range(SIDE):
        experts = local_experts("z", k)
        gains = parts[k][LANES : LANES + 8, 0 : 3 * LANES].astype(F32)
        gains = (gains[:, :LANES] + gains[:, LANES : 2 * LANES]) + gains[:, 2 * LANES :]
        for j in range(TOP):
            hit = ids[j : j + 1, :] == experts
            total[j] = total[j] + jnp.sum(jnp.where(hit, gains, 0.0), axis=0, keepdims=True)
    total = [total[j] / gate[j : j + 1, :] for j in range(TOP)]
    gate_out[...] = jnp.concatenate(total, axis=0)


def forward_body(count, *refs):
    blocks, (gate_t, up_t, down) = refs[:count], refs[count : count + 3]
    outs = refs[count + 3 : 2 * count + 3]
    gate_factor_out, silu_out, act_out = refs[2 * count + 3 :]
    rows = jnp.concatenate([b[...] for b in blocks], axis=0)
    gate_pre = contract_lanes(rows, gate_t[...])
    up_pre = contract_lanes(rows, up_t[...])
    sigmoid_val = jax.nn.sigmoid(gate_pre)
    silu_val = gate_pre * sigmoid_val
    gate_factor_out[...] = (up_pre * sigmoid_val * (1.0 + gate_pre * (1.0 - sigmoid_val))).astype(BF16)
    silu_out[...] = silu_val.astype(BF16)
    act_out[...] = (silu_val * up_pre).astype(BF16)

    def column(n, carry):
        at = pl.ds(pl.multiple_of(n * TILE, TILE), TILE)
        result = jnp.dot(act_out[...], down[:, at], preferred_element_type=F32).astype(BF16)
        for i in range(count):
            outs[i][:, at] = result[i * ROWS : (i + 1) * ROWS, :]
        return carry

    lax.fori_loop(0, down.shape[1] // TILE, column, 0)


def hidden_slices(counts):
    place = {}
    for n, ks in enumerate(counts):
        for i, k in enumerate(ks):
            for flip in range(CORES):
                place[2 * k + flip] = (n, (2 * i + flip) * ROWS)
    return place


def backward_body(kzs, place, arrays, *refs):
    count = 2 * len(kzs)
    cots, refs = refs[:count], refs[count:]
    factors, silus, acts, refs = refs[:arrays], refs[arrays : 2 * arrays], refs[2 * arrays : 3 * arrays], refs[3 * arrays :]
    (gate_t, up_t, down), refs = refs[:3], refs[3:]
    outs, gate_grad_out, up_grad_out = refs[:count], refs[count], refs[count + 1]

    def ordered(parts):
        pieces = []
        for kz in kzs:
            for flip in range(CORES):
                for kx in range(SIDE):
                    n, first = place[2 * kx + flip]
                    pieces.append(parts[n][first + kz * CAP : first + (kz + 1) * CAP, :])
        return jnp.concatenate(pieces, axis=0)

    cot = jnp.concatenate([c[...] for c in cots], axis=0)
    act_grad = contract_lanes(cot, down[...])
    gate_grad_out[...] = (act_grad * ordered(factors).astype(F32)).astype(BF16)
    up_grad_out[...] = (act_grad * ordered(silus).astype(F32)).astype(BF16)
    product = jnp.sum(ordered(acts).astype(F32) * act_grad, axis=1, keepdims=True)
    width = down.shape[1]
    for n in range(count):
        part = jnp.broadcast_to(product[n * ROWS : (n + 1) * ROWS, :], (ROWS, LANES))
        part = jnp.transpose(part)[0:8, :]
        outs[n][ROWS : ROWS + 8, 0 : 3 * LANES] = jnp.concatenate(thirds(part), axis=1)
        outs[n][ROWS : ROWS + 8, 3 * LANES :] = jnp.zeros((8, width - 3 * LANES), BF16)

    def column(n, carry):
        at = pl.ds(pl.multiple_of(n * TILE, TILE), TILE)
        result = (
            jnp.dot(gate_grad_out[...], gate_t[:, at], preferred_element_type=F32)
            + jnp.dot(up_grad_out[...], up_t[:, at], preferred_element_type=F32)
        ).astype(BF16)
        for i in range(count):
            outs[i][0:ROWS, at] = result[i * ROWS : (i + 1) * ROWS, :]
        return carry

    lax.fori_loop(0, width // TILE, column, 0)


def in_cot_order(blocks, columns, kzs):
    return jnp.concatenate(
        [
            blocks[2 * kx + flip][kz * CAP : (kz + 1) * CAP, columns]
            for kz in kzs
            for flip in range(CORES)
            for kx in range(SIDE)
        ],
        axis=0,
    )


def column_grad_body(order, arrays, *refs):
    gates, ups, blocks = refs[:arrays], refs[arrays : 2 * arrays], refs[2 * arrays : 2 * arrays + 8]
    own, ahead, behind, ahead_kept, behind_kept, turned, piece = refs[2 * arrays + 8 :]
    rep = lax.axis_index("rep")
    width = own.shape[1]
    hidden = gates[0].shape[1]
    turned[0] = jnp.transpose(jnp.concatenate([h[...] for h in gates], axis=0))
    turned[1] = jnp.transpose(jnp.concatenate([h[...] for h in ups], axis=0))
    places = ((own.at[0:hidden, :], own.at[hidden:, :]), (ahead_kept, ahead.at[0:hidden, :]),
              (ahead.at[hidden:, :], behind.at[hidden:, :]), (behind.at[0:hidden, :], behind_kept))

    def chunk(k, carry):
        start = pl.multiple_of(((rep + k) & 3) * width, LANES)
        right = in_cot_order(blocks, pl.ds(start, width), order)
        for half in range(2):
            piece[half] = jnp.dot(turned[half], right, preferred_element_type=F32).astype(BF16)
        for n in range(4):

            @pl.when(k == n)
            def _():
                for half in range(2):
                    places[n][half][...] = piece[half]

        return carry

    lax.fori_loop(0, 4, chunk, 0)


def row_grad_body(place, arrays, *refs):
    acts, blocks = refs[:arrays], refs[arrays : arrays + 8]
    own, ahead, behind, ahead_kept, behind_kept, turned, whole = refs[arrays + 8 :]
    rep = lax.axis_index("rep")
    height, width = own.shape
    half = width // 2
    pieces = []
    for kz in range(SIDE):
        for flip in range(CORES):
            for kx in range(SIDE):
                n, first = place[2 * kx + flip]
                pieces.append(acts[n][first + kz * CAP : first + (kz + 1) * CAP, :])
    turned[...] = jnp.transpose(jnp.concatenate(pieces, axis=0))

    def column(n, carry):
        at = pl.ds(pl.multiple_of(n * TILE, TILE), TILE)
        right = jnp.concatenate([b[:, at] for b in blocks], axis=0)
        whole[:, at] = jnp.dot(turned[...], right, preferred_element_type=F32).astype(BF16)
        return carry

    lax.fori_loop(0, width // TILE, column, 0)

    def rows_for(k):
        return pl.ds(pl.multiple_of(((rep + k) & 3) * height, 16), height)

    own[...] = whole[rows_for(0), :]
    ahead_kept[...] = whole[rows_for(1), 0:half]
    ahead[:, 0:half] = whole[rows_for(1), half:]
    ahead[:, half:] = whole[rows_for(2), 0:half]
    behind[:, 0:half] = whole[rows_for(3), 0:half]
    behind[:, half:] = whole[rows_for(2), half:]
    behind_kept[...] = whole[rows_for(3), half:]


def relay_body(axis, from_behind, from_ahead, ahead_kept, behind_kept, ahead_out, behind_out):
    far = slice(ahead_kept.shape[axis], None)
    at = (far, slice(None)) if axis == 0 else (slice(None), far)
    ahead_out[...] = (from_behind[at].astype(F32) + ahead_kept[...].astype(F32)).astype(BF16)
    behind_out[...] = (from_ahead[at].astype(F32) + behind_kept[...].astype(F32)).astype(BF16)


def call(body, args, outs, flops, scratch=(), limit=14, outside=False):
    moved = sum(a.size * a.dtype.itemsize for a in args) + sum(
        o.size * o.dtype.itemsize for o in outs
    )
    vmem = pl.BlockSpec(memory_space=pltpu.VMEM)
    return pl.pallas_call(
        body,
        out_shape=tuple(outs),
        in_specs=[pl.BlockSpec(memory_space=pltpu.HBM) if outside else vmem] * len(args),
        out_specs=tuple([vmem] * len(outs)),
        scratch_shapes=list(scratch),
        cost_estimate=pl.CostEstimate(flops=flops, bytes_accessed=moved, transcendentals=0),
        compiler_params=pltpu.CompilerParams(vmem_limit_bytes=limit * 1024 * 1024),
    )(*args)


def per_device(tokens, expert_ids, gate_weights, cotangent, w_gate, w_up, w_down):
    tok_rows, width = tokens.shape
    gate_t = jnp.swapaxes(w_gate[0], 0, 1)
    up_t = jnp.swapaxes(w_up[0], 0, 1)
    down = w_down[0]
    hidden = down.shape[0]

    def block(dtype=BF16, rows=ROWS, columns=width):
        return jax.ShapeDtypeStruct((rows, columns), dtype)

    tall = block(BF16, ROWS + 8)
    packed_tokens, packed_cot = call(
        pack_body, [tokens, cotangent, expert_ids.T, gate_weights.T], [tall] * 2, 0,
        [pltpu.VMEM((TOP, tok_rows), jnp.int32), pltpu.VMEM((TOP, tok_rows), F32),
         pltpu.SemaphoreType.DMA((4,))],
        limit=4, outside=True,
    )
    hops = (1, 3, 2)
    token_parts, cot_parts = {0: packed_tokens}, {0: packed_cot}
    for k in hops:
        token_parts[k] = move(packed_tokens, "z", k, 0)
        cot_parts[k] = move(packed_cot, "x", k, 0)

    def four(parts):
        return [parts[k] for k in range(SIDE)]

    from_z, from_x = four(token_parts), four(cot_parts)
    gather_flops = 2 * DESTS * ROWS * LANES * width
    sent = call(
        functools.partial(dispatch_body, "x", False), from_z, [block()] * DESTS, gather_flops,
        limit=10,
    )
    sent_cot = call(
        functools.partial(dispatch_body, "z", True), from_x, [block()] * DESTS, gather_flops,
        limit=10,
    )
    rows = [move(sent[q], "x", q >> 1, q & 1) for q in range(DESTS)]
    cots = [move(sent_cot[q], "z", q >> 1, q & 1) for q in range(DESTS)]

    unit = 2 * ROWS * width * hidden
    groups = ((0,), (1, 3), (2,))
    place = hidden_slices(groups)
    out_blocks, gates, ups, acts = {}, [], [], []
    for ks in groups:
        qs = [2 * k + flip for k in ks for flip in range(CORES)]
        count = len(qs)
        results = call(
            functools.partial(forward_body, count),
            [rows[q] for q in qs] + [gate_t, up_t, down],
            [block()] * count + [block(BF16, count * ROWS, hidden)] * 3,
            3 * count * unit, limit=9,
        )
        for q, value in zip(qs, results):
            out_blocks[q] = value
        gates.append(results[count])
        ups.append(results[count + 1])
        acts.append(results[count + 2])
    out_back = [move(out_blocks[q], "x", -(q >> 1), q & 1) for q in range(DESTS)]

    back_groups = ((1, 3), (2, 0))
    row_blocks, gate_grads, up_grads = {}, [], []
    for ks in back_groups:
        qs = [2 * k + flip for k in ks for flip in range(CORES)]
        count = len(qs)
        results = call(
            functools.partial(backward_body, ks, place, len(groups)),
            [cots[q] for q in qs] + gates + ups + acts + [gate_t, up_t, down],
            [tall] * count + [block(BF16, count * ROWS, hidden)] * 2,
            3 * count * unit, limit=11,
        )
        for q, value in zip(qs, results):
            row_blocks[q] = value
        gate_grads.append(results[count])
        up_grads.append(results[count + 1])
    rows_back = [move(row_blocks[q], "z", -(q >> 1), q & 1) for q in range(DESTS)]

    order = tuple(k for ks in back_groups for k in ks)

    def chunks(rows_, columns, axis):
        halved = (rows_ // 2, columns) if axis == 0 else (rows_, columns // 2)
        return [block(BF16, rows_, columns)] * 3 + [block(BF16, *halved)] * 2

    down_parts = call(
        functools.partial(row_grad_body, place, len(groups)), acts + cots,
        chunks(hidden // 4, width, 1), 8 * unit,
        [pltpu.VMEM((hidden, DESTS * ROWS), BF16), pltpu.VMEM((hidden, width), BF16)],
    )
    both_parts = call(
        functools.partial(column_grad_body, order, len(back_groups)),
        gate_grads + up_grads + rows, chunks(2 * hidden, width // 4, 0), 16 * unit,
        [pltpu.VMEM((2, hidden, DESTS * ROWS), BF16), pltpu.VMEM((2, hidden, width // 4), BF16)],
    )

    def pass_on(value, step):
        return lax.ppermute(value, "rep", [(r, (r + step) % 4) for r in range(4)])

    def reduced(parts, axis):
        own, ahead, behind, ahead_kept, behind_kept = parts
        from_behind = pass_on(ahead, 1)
        from_ahead = pass_on(behind, 3)
        ahead, behind = call(
            functools.partial(relay_body, axis),
            [from_behind, from_ahead, ahead_kept, behind_kept],
            [jax.ShapeDtypeStruct(ahead_kept.shape, BF16)] * 2, ahead_kept.size,
            limit=8,
        )
        relayed_behind = pass_on(ahead, 1)
        relayed_ahead = pass_on(behind, 3)

        def halves(value):
            return [h.astype(F32) for h in jnp.split(value, 2, axis=axis)]

        (own_a, own_b), near_b, near_a = halves(own), halves(from_behind)[0], halves(from_ahead)[0]
        return (
            own_a + near_a + relayed_behind.astype(F32), own_b + near_b + relayed_ahead.astype(F32)
        )

    grad_down = jnp.concatenate(reduced(down_parts, 1), axis=1)[None]
    grad_gate, grad_up = [jnp.swapaxes(g, 0, 1)[None] for g in reduced(both_parts, 0)]

    mixed_parts = call(
        combine_out_body, out_back + from_z, [block()] * SIDE, 2 * gather_flops,
        limit=10,
    )
    mixed_parts = [move(mixed_parts[s], "z", -s, 0) for s in range(SIDE)]
    (mixed,) = call(sum_parts_body, mixed_parts, [block()], 4 * tok_rows * width, limit=4)

    grad_parts = call(combine_grad_body, rows_back + from_x, [tall] * SIDE, gather_flops, limit=10)
    grad_parts = [move(grad_parts[s], "x", -s, 0) for s in range(SIDE)]
    token_grad, gate_grad = call(
        finish_grad_body, grad_parts + [packed_tokens],
        [block(), block(F32, TOP, LANES)], 4 * tok_rows * width, limit=8,
    )
    return (mixed, token_grad, gate_grad.T, grad_gate, grad_up, grad_down)


def solution(mesh):
    placed = (
        P(("rep", "ep"), None),
        P(("rep", "ep"), None),
        P(("rep", "ep"), None),
        P(("rep", "ep"), None),
        P("ep", None, None),
        P("ep", None, None),
        P("ep", None, None),
    )

    return jax.shard_map(
        per_device,
        mesh=mesh,
        in_specs=placed,
        out_specs=(
            P(("rep", "ep"), None),
            P(("rep", "ep"), None),
            P(("rep", "ep"), None),
            P("ep", "rep", None),
            P("ep", "rep", None),
            P("ep", "rep", None),
        ),
        check_vma=False,
    )
```

```python
import functools

import jax
import jax.numpy as jnp
from jax import lax
from jax.experimental import pallas as pl
from jax.experimental.pallas import tpu as pltpu
from jax.sharding import PartitionSpec as P


F32 = jnp.float32
BF16 = jnp.bfloat16
SIDE = 4
CORES = 2
LANES = 128
CAP = 32
TOP = 6
DESTS = SIDE * CORES
TILE = 512
WIDE = 1024
ROWS = SIDE * CAP


def device_of(z, x, c):
    return (z % SIDE) * SIDE * CORES + (x % SIDE) * CORES + c


def shift_pairs(axis, step, flip):
    pairs = []
    for z in range(SIDE):
        for x in range(SIDE):
            for c in range(CORES):
                there = device_of(z, x + step, c ^ flip) if axis == "x" else device_of(z + step, x, c ^ flip)
                pairs.append((device_of(z, x, c), there))
    return pairs


def move(value, axis, step, flip=0):
    if step % SIDE == 0 and flip == 0:
        return value
    return lax.ppermute(value, "ep", shift_pairs(axis, step, flip))


def position():
    at = lax.axis_index("ep")
    return at >> 3, (at >> 1) & 3, at & 1


def local_experts(axis, offset=0):
    z, x, c = position()
    q = lax.broadcasted_iota(jnp.int32, (DESTS, LANES), 0)
    k, flip = q >> 1, q & 1
    core = (c + flip) & 1
    if axis == "x":
        ids = (z << 3) + (((x + k) & 3) << 1) + core
    else:
        ids = (((z + k) & 3) << 3) + (((x + offset) & 3) << 1) + core
    return ids.astype(F32)


def thirds(value):
    high = value.astype(BF16)
    rest = value - high.astype(F32)
    mid = rest.astype(BF16)
    return high, mid, (rest - mid.astype(F32)).astype(BF16)


def selection(meta, experts):
    ids, gate = meta[0:TOP, :], meta[8 : 8 + TOP, :]
    named = jnp.zeros((DESTS, LANES), F32)
    weight = jnp.zeros((DESTS, LANES), F32)
    for j in range(TOP):
        hit = ids[j : j + 1, :] == experts
        named = named + jnp.where(hit, 1.0, 0.0)
        weight = weight + jnp.where(hit, gate[j : j + 1, :], 0.0)
    earlier = lax.broadcasted_iota(jnp.int32, (LANES, LANES), 0) < lax.broadcasted_iota(
        jnp.int32, (LANES, LANES), 1
    )
    before = jnp.dot(
        named.astype(BF16), jnp.where(earlier, 1.0, 0.0).astype(BF16), preferred_element_type=F32
    )
    place = jnp.where(named > 0.5, before, -1.0)
    slot = lax.broadcasted_iota(jnp.int32, (CAP, LANES), 0).astype(F32)
    chosen = jnp.concatenate(
        [
            jnp.where(jnp.broadcast_to(place[q : q + 1, :], (CAP, LANES)) == slot, 1.0, 0.0)
            for q in range(DESTS)
        ],
        axis=0,
    )
    spread = jnp.concatenate(
        [jnp.broadcast_to(weight[q : q + 1, :], (CAP, LANES)) for q in range(DESTS)], axis=0
    )
    return chosen, spread


def dispatch_body(axis, scaled, *refs):
    sources, metas, outs = refs[:4], refs[4:8], refs[8:]
    experts = local_experts(axis)
    for s in range(SIDE):
        chosen, spread = selection(metas[s], experts)
        scale = jnp.sum(chosen * spread, axis=1, keepdims=True) if scaled else None
        chosen = chosen.astype(BF16)

        def column(n, carry, s=s, chosen=chosen, scale=scale):
            at = pl.ds(pl.multiple_of(n * WIDE, WIDE), WIDE)
            rows = jnp.dot(chosen, sources[s][:, at], preferred_element_type=F32)
            if scaled:
                rows = rows * scale
            rows = rows.astype(BF16)
            for q in range(DESTS):
                outs[q][s * CAP : (s + 1) * CAP, at] = rows[q * CAP : (q + 1) * CAP, :]
            return carry

        lax.fori_loop(0, outs[0].shape[1] // WIDE, column, 0)


def contract_rows(left, right):
    return lax.dot_general(left, right, (((0,), (0,)), ((), ())), preferred_element_type=F32)


def contract_lanes(left, right):
    return lax.dot_general(left, right, (((1,), (1,)), ((), ())), preferred_element_type=F32)


def source_rows(blocks, s, columns):
    return jnp.concatenate(
        [blocks[q][s * CAP : (s + 1) * CAP, columns] for q in range(DESTS)], axis=0
    )


def combine_out_body(*refs):
    blocks, metas, outs = refs[:8], refs[8:12], refs[12:]
    experts = local_experts("x")
    for s in range(SIDE):
        chosen, spread = selection(metas[s], experts)
        mix = chosen * spread
        high = mix.astype(BF16)
        mix = jnp.concatenate([high, (mix - high.astype(F32)).astype(BF16)], axis=1)

        def column(n, carry, s=s, mix=mix):
            at = pl.ds(pl.multiple_of(n * TILE, TILE), TILE)
            both = contract_rows(mix, source_rows(blocks, s, at))
            outs[s][:, at] = (both[:LANES, :] + both[LANES:, :]).astype(BF16)
            return carry

        lax.fori_loop(0, outs[0].shape[1] // TILE, column, 0)


def combine_grad_body(*refs):
    blocks, metas, outs = refs[:8], refs[8:12], refs[12:]
    experts = local_experts("z")
    columns = []
    for q in range(DESTS):
        product = blocks[q][ROWS : ROWS + 8, 0 : 3 * LANES].astype(F32)
        product = (product[:, :LANES] + product[:, LANES : 2 * LANES]) + product[:, 2 * LANES :]
        columns.append(jnp.transpose(jnp.broadcast_to(product[0:1, :], (LANES, LANES))))
    for s in range(SIDE):
        chosen, _ = selection(metas[s], experts)
        picked = chosen.astype(BF16)

        def column(n, carry, s=s, picked=picked):
            at = pl.ds(pl.multiple_of(n * TILE, TILE), TILE)
            outs[s][0:LANES, at] = contract_rows(picked, source_rows(blocks, s, at)).astype(BF16)
            return carry

        width = outs[0].shape[1]
        lax.fori_loop(0, width // TILE, column, 0)
        gains = jnp.concatenate(
            [
                jnp.sum(
                    chosen[q * CAP : (q + 1) * CAP, :] * columns[q][s * CAP : (s + 1) * CAP, :],
                    axis=0,
                    keepdims=True,
                )
                for q in range(DESTS)
            ],
            axis=0,
        )
        outs[s][LANES : LANES + 8, 0 : 3 * LANES] = jnp.concatenate(thirds(gains), axis=1)
        outs[s][LANES : LANES + 8, 3 * LANES :] = jnp.zeros((8, width - 3 * LANES), BF16)


def sum_parts_body(*refs):
    parts, out = refs[:4], refs[4]
    out[...] = (
        (parts[0][...].astype(F32) + parts[1][...].astype(F32))
        + (parts[2][...].astype(F32) + parts[3][...].astype(F32))
    ).astype(BF16)


def finish_grad_body(*refs):
    parts, meta, out, gate_out = refs[:4], refs[4], refs[5], refs[6]
    sum_parts_body(*[p.at[0:LANES, :] for p in parts], out)
    ids, gate = meta[0:TOP, :], meta[8 : 8 + TOP, :]
    total = [jnp.zeros((1, LANES), F32) for _ in range(TOP)]
    for k in range(SIDE):
        experts = local_experts("z", k)
        gains = parts[k][LANES : LANES + 8, 0 : 3 * LANES].astype(F32)
        gains = (gains[:, :LANES] + gains[:, LANES : 2 * LANES]) + gains[:, 2 * LANES :]
        for j in range(TOP):
            hit = ids[j : j + 1, :] == experts
            total[j] = total[j] + jnp.sum(jnp.where(hit, gains, 0.0), axis=0, keepdims=True)
    total = [total[j] / gate[j : j + 1, :] for j in range(TOP)]
    gate_out[...] = jnp.concatenate(total, axis=0)


def forward_body(count, *refs):
    blocks, (gate_t, up_t, down) = refs[:count], refs[count : count + 3]
    outs = refs[count + 3 : 2 * count + 3]
    gate_factor_out, silu_out, act_out = refs[2 * count + 3 :]
    rows = jnp.concatenate([b[...] for b in blocks], axis=0)
    gate_pre = contract_lanes(rows, gate_t[...])
    up_pre = contract_lanes(rows, up_t[...])
    sigmoid_val = jax.nn.sigmoid(gate_pre)
    silu_val = gate_pre * sigmoid_val
    gate_factor_out[...] = (up_pre * sigmoid_val * (1.0 + gate_pre * (1.0 - sigmoid_val))).astype(BF16)
    silu_out[...] = silu_val.astype(BF16)
    act_out[...] = (silu_val * up_pre).astype(BF16)

    def column(n, carry):
        at = pl.ds(pl.multiple_of(n * TILE, TILE), TILE)
        result = jnp.dot(act_out[...], down[:, at], preferred_element_type=F32).astype(BF16)
        for i in range(count):
            outs[i][:, at] = result[i * ROWS : (i + 1) * ROWS, :]
        return carry

    lax.fori_loop(0, down.shape[1] // TILE, column, 0)


def hidden_slices(counts):
    place = {}
    for n, ks in enumerate(counts):
        for i, k in enumerate(ks):
            for flip in range(CORES):
                place[2 * k + flip] = (n, (2 * i + flip) * ROWS)
    return place


def backward_body(kzs, place, arrays, *refs):
    count = 2 * len(kzs)
    cots, refs = refs[:count], refs[count:]
    factors, silus, acts, refs = refs[:arrays], refs[arrays : 2 * arrays], refs[2 * arrays : 3 * arrays], refs[3 * arrays :]
    (gate_t, up_t, down), refs = refs[:3], refs[3:]
    outs, gate_grad_out, up_grad_out = refs[:count], refs[count], refs[count + 1]

    def ordered(parts):
        pieces = []
        for kz in kzs:
            for flip in range(CORES):
                for kx in range(SIDE):
                    n, first = place[2 * kx + flip]
                    pieces.append(parts[n][first + kz * CAP : first + (kz + 1) * CAP, :])
        return jnp.concatenate(pieces, axis=0)

    cot = jnp.concatenate([c[...] for c in cots], axis=0)
    act_grad = contract_lanes(cot, down[...])
    gate_grad_out[...] = (act_grad * ordered(factors).astype(F32)).astype(BF16)
    up_grad_out[...] = (act_grad * ordered(silus).astype(F32)).astype(BF16)
    product = jnp.sum(ordered(acts).astype(F32) * act_grad, axis=1, keepdims=True)
    width = down.shape[1]
    for n in range(count):
        part = jnp.broadcast_to(product[n * ROWS : (n + 1) * ROWS, :], (ROWS, LANES))
        part = jnp.transpose(part)[0:8, :]
        outs[n][ROWS : ROWS + 8, 0 : 3 * LANES] = jnp.concatenate(thirds(part), axis=1)
        outs[n][ROWS : ROWS + 8, 3 * LANES :] = jnp.zeros((8, width - 3 * LANES), BF16)

    def column(n, carry):
        at = pl.ds(pl.multiple_of(n * TILE, TILE), TILE)
        result = (
            jnp.dot(gate_grad_out[...], gate_t[:, at], preferred_element_type=F32)
            + jnp.dot(up_grad_out[...], up_t[:, at], preferred_element_type=F32)
        ).astype(BF16)
        for i in range(count):
            outs[i][0:ROWS, at] = result[i * ROWS : (i + 1) * ROWS, :]
        return carry

    lax.fori_loop(0, width // TILE, column, 0)


def in_cot_order(blocks, columns, kzs):
    return jnp.concatenate(
        [
            blocks[2 * kx + flip][kz * CAP : (kz + 1) * CAP, columns]
            for kz in kzs
            for flip in range(CORES)
            for kx in range(SIDE)
        ],
        axis=0,
    )


def column_grad_body(order, arrays, *refs):
    gates, ups, blocks = refs[:arrays], refs[arrays : 2 * arrays], refs[2 * arrays : 2 * arrays + 8]
    own, ahead, behind, ahead_kept, behind_kept, turned, piece = refs[2 * arrays + 8 :]
    rep = lax.axis_index("rep")
    width = own.shape[1]
    hidden = gates[0].shape[1]
    turned[0] = jnp.transpose(jnp.concatenate([h[...] for h in gates], axis=0))
    turned[1] = jnp.transpose(jnp.concatenate([h[...] for h in ups], axis=0))
    places = ((own.at[0:hidden, :], own.at[hidden:, :]), (ahead_kept, ahead.at[0:hidden, :]),
              (ahead.at[hidden:, :], behind.at[hidden:, :]), (behind.at[0:hidden, :], behind_kept))

    def chunk(k, carry):
        start = pl.multiple_of(((rep + k) & 3) * width, LANES)
        right = in_cot_order(blocks, pl.ds(start, width), order)
        for half in range(2):
            piece[half] = jnp.dot(turned[half], right, preferred_element_type=F32).astype(BF16)
        for n in range(4):

            @pl.when(k == n)
            def _():
                for half in range(2):
                    places[n][half][...] = piece[half]

        return carry

    lax.fori_loop(0, 4, chunk, 0)


def row_grad_body(place, arrays, *refs):
    acts, blocks = refs[:arrays], refs[arrays : arrays + 8]
    own, ahead, behind, ahead_kept, behind_kept, turned, whole = refs[arrays + 8 :]
    rep = lax.axis_index("rep")
    height, width = own.shape
    half = width // 2
    pieces = []
    for kz in range(SIDE):
        for flip in range(CORES):
            for kx in range(SIDE):
                n, first = place[2 * kx + flip]
                pieces.append(acts[n][first + kz * CAP : first + (kz + 1) * CAP, :])
    turned[...] = jnp.transpose(jnp.concatenate(pieces, axis=0))

    def column(n, carry):
        at = pl.ds(pl.multiple_of(n * TILE, TILE), TILE)
        right = jnp.concatenate([b[:, at] for b in blocks], axis=0)
        whole[:, at] = jnp.dot(turned[...], right, preferred_element_type=F32).astype(BF16)
        return carry

    lax.fori_loop(0, width // TILE, column, 0)

    def rows_for(k):
        return pl.ds(pl.multiple_of(((rep + k) & 3) * height, 16), height)

    own[...] = whole[rows_for(0), :]
    ahead_kept[...] = whole[rows_for(1), 0:half]
    ahead[:, 0:half] = whole[rows_for(1), half:]
    ahead[:, half:] = whole[rows_for(2), 0:half]
    behind[:, 0:half] = whole[rows_for(3), 0:half]
    behind[:, half:] = whole[rows_for(2), half:]
    behind_kept[...] = whole[rows_for(3), half:]


def relay_body(axis, from_behind, from_ahead, ahead_kept, behind_kept, ahead_out, behind_out):
    far = slice(ahead_kept.shape[axis], None)
    at = (far, slice(None)) if axis == 0 else (slice(None), far)
    ahead_out[...] = (from_behind[at].astype(F32) + ahead_kept[...].astype(F32)).astype(BF16)
    behind_out[...] = (from_ahead[at].astype(F32) + behind_kept[...].astype(F32)).astype(BF16)


def call(body, args, outs, flops, scratch=(), limit=14):
    moved = sum(a.size * a.dtype.itemsize for a in args) + sum(
        o.size * o.dtype.itemsize for o in outs
    )
    vmem = pl.BlockSpec(memory_space=pltpu.VMEM)
    return pl.pallas_call(
        body,
        out_shape=tuple(outs),
        in_specs=[vmem] * len(args),
        out_specs=tuple([vmem] * len(outs)),
        scratch_shapes=list(scratch),
        cost_estimate=pl.CostEstimate(flops=flops, bytes_accessed=moved, transcendentals=0),
        compiler_params=pltpu.CompilerParams(vmem_limit_bytes=limit * 1024 * 1024),
    )(*args)


def per_device(tokens, expert_ids, gate_weights, cotangent, w_gate, w_up, w_down):
    tok_rows, width = tokens.shape
    gate_t = jnp.swapaxes(w_gate[0], 0, 1)
    up_t = jnp.swapaxes(w_up[0], 0, 1)
    down = w_down[0]
    hidden = down.shape[0]

    def block(dtype=BF16, rows=ROWS, columns=width):
        return jax.ShapeDtypeStruct((rows, columns), dtype)

    tall = block(BF16, ROWS + 8)
    pad = jnp.zeros((2, tok_rows), F32)
    meta = jnp.concatenate([expert_ids.T.astype(F32), pad, gate_weights.T, pad], axis=0)
    hops = (1, 3, 2)
    token_parts, cot_parts = {0: tokens}, {0: cotangent}
    meta_z, meta_x = {0: meta}, {0: meta}
    for k in hops:
        token_parts[k] = move(tokens, "z", k, 0)
        cot_parts[k] = move(cotangent, "x", k, 0)
        meta_z[k] = move(meta, "z", k, 0)
        meta_x[k] = move(meta, "x", k, 0)

    def four(parts):
        return [parts[k] for k in range(SIDE)]

    from_z, from_x = four(token_parts) + four(meta_z), four(cot_parts) + four(meta_x)
    gather_flops = 2 * DESTS * ROWS * LANES * width
    sent = call(
        functools.partial(dispatch_body, "x", False), from_z, [block()] * DESTS, gather_flops,
        limit=10,
    )
    sent_cot = call(
        functools.partial(dispatch_body, "z", True), from_x, [block()] * DESTS, gather_flops,
        limit=10,
    )
    rows = [move(sent[q], "x", q >> 1, q & 1) for q in range(DESTS)]
    cots = [move(sent_cot[q], "z", q >> 1, q & 1) for q in range(DESTS)]

    unit = 2 * ROWS * width * hidden
    groups = ((0,), (1, 3), (2,))
    place = hidden_slices(groups)
    out_blocks, gates, ups, acts = {}, [], [], []
    for ks in groups:
        qs = [2 * k + flip for k in ks for flip in range(CORES)]
        count = len(qs)
        results = call(
            functools.partial(forward_body, count),
            [rows[q] for q in qs] + [gate_t, up_t, down],
            [block()] * count + [block(BF16, count * ROWS, hidden)] * 3,
            3 * count * unit, limit=9,
        )
        for q, value in zip(qs, results):
            out_blocks[q] = value
        gates.append(results[count])
        ups.append(results[count + 1])
        acts.append(results[count + 2])
    out_back = [move(out_blocks[q], "x", -(q >> 1), q & 1) for q in range(DESTS)]

    back_groups = ((1, 3), (2, 0))
    row_blocks, gate_grads, up_grads = {}, [], []
    for ks in back_groups:
        qs = [2 * k + flip for k in ks for flip in range(CORES)]
        count = len(qs)
        results = call(
            functools.partial(backward_body, ks, place, len(groups)),
            [cots[q] for q in qs] + gates + ups + acts + [gate_t, up_t, down],
            [tall] * count + [block(BF16, count * ROWS, hidden)] * 2,
            3 * count * unit, limit=11,
        )
        for q, value in zip(qs, results):
            row_blocks[q] = value
        gate_grads.append(results[count])
        up_grads.append(results[count + 1])
    rows_back = [move(row_blocks[q], "z", -(q >> 1), q & 1) for q in range(DESTS)]

    order = tuple(k for ks in back_groups for k in ks)

    def chunks(rows_, columns, axis):
        halved = (rows_ // 2, columns) if axis == 0 else (rows_, columns // 2)
        return [block(BF16, rows_, columns)] * 3 + [block(BF16, *halved)] * 2

    down_parts = call(
        functools.partial(row_grad_body, place, len(groups)), acts + cots,
        chunks(hidden // 4, width, 1), 8 * unit,
        [pltpu.VMEM((hidden, DESTS * ROWS), BF16), pltpu.VMEM((hidden, width), BF16)],
    )
    both_parts = call(
        functools.partial(column_grad_body, order, len(back_groups)),
        gate_grads + up_grads + rows, chunks(2 * hidden, width // 4, 0), 16 * unit,
        [pltpu.VMEM((2, hidden, DESTS * ROWS), BF16), pltpu.VMEM((2, hidden, width // 4), BF16)],
    )

    def pass_on(value, step):
        return lax.ppermute(value, "rep", [(r, (r + step) % 4) for r in range(4)])

    def reduced(parts, axis):
        own, ahead, behind, ahead_kept, behind_kept = parts
        from_behind = pass_on(ahead, 1)
        from_ahead = pass_on(behind, 3)
        ahead, behind = call(
            functools.partial(relay_body, axis),
            [from_behind, from_ahead, ahead_kept, behind_kept],
            [jax.ShapeDtypeStruct(ahead_kept.shape, BF16)] * 2, ahead_kept.size,
            limit=8,
        )
        relayed_behind = pass_on(ahead, 1)
        relayed_ahead = pass_on(behind, 3)

        def halves(value):
            return [h.astype(F32) for h in jnp.split(value, 2, axis=axis)]

        (own_a, own_b), near_b, near_a = halves(own), halves(from_behind)[0], halves(from_ahead)[0]
        return (
            own_a + near_a + relayed_behind.astype(F32), own_b + near_b + relayed_ahead.astype(F32)
        )

    grad_down = jnp.concatenate(reduced(down_parts, 1), axis=1)[None]
    grad_gate, grad_up = [jnp.swapaxes(g, 0, 1)[None] for g in reduced(both_parts, 0)]

    mixed_parts = call(
        combine_out_body, out_back + from_z[4:], [block()] * SIDE, 2 * gather_flops,
        limit=10,
    )
    mixed_parts = [move(mixed_parts[s], "z", -s, 0) for s in range(SIDE)]
    (mixed,) = call(sum_parts_body, mixed_parts, [block()], 4 * tok_rows * width, limit=4)

    grad_parts = call(
        combine_grad_body, rows_back + from_x[4:], [tall] * SIDE, gather_flops, limit=10,
    )
    grad_parts = [move(grad_parts[s], "x", -s, 0) for s in range(SIDE)]
    token_grad, gate_grad = call(
        finish_grad_body, grad_parts + [meta],
        [block(), block(F32, TOP, LANES)], 4 * tok_rows * width, limit=8,
    )
    return (mixed, token_grad, gate_grad.T, grad_gate, grad_up, grad_down)


def solution(mesh):
    placed = (
        P(("rep", "ep"), None),
        P(("rep", "ep"), None),
        P(("rep", "ep"), None),
        P(("rep", "ep"), None),
        P("ep", None, None),
        P("ep", None, None),
        P("ep", None, None),
    )

    return jax.shard_map(
        per_device,
        mesh=mesh,
        in_specs=placed,
        out_specs=(
            P(("rep", "ep"), None),
            P(("rep", "ep"), None),
            P(("rep", "ep"), None),
            P("ep", "rep", None),
            P("ep", "rep", None),
            P("ep", "rep", None),
        ),
        check_vma=False,
    )
```

```python
import functools

import jax
import jax.numpy as jnp
from jax import lax
from jax.experimental import pallas as pl
from jax.experimental.pallas import tpu as pltpu
from jax.sharding import PartitionSpec as P


F32 = jnp.float32
BF16 = jnp.bfloat16
SIDE = 4
CORES = 2
LANES = 128
CAP = 32
TOP = 6
DESTS = SIDE * CORES
TILE = 512
NARROW = 256
WIDE = 1024
ROWS = SIDE * CAP


def device_of(z, x, c):
    return (z % SIDE) * SIDE * CORES + (x % SIDE) * CORES + c


def shift_pairs(axis, step, flip):
    pairs = []
    for z in range(SIDE):
        for x in range(SIDE):
            for c in range(CORES):
                there = device_of(z, x + step, c ^ flip) if axis == "x" else device_of(z + step, x, c ^ flip)
                pairs.append((device_of(z, x, c), there))
    return pairs


def move(value, axis, step, flip=0):
    if step % SIDE == 0 and flip == 0:
        return value
    return lax.ppermute(value, "ep", shift_pairs(axis, step, flip))


def position():
    at = lax.axis_index("ep")
    return at >> 3, (at >> 1) & 3, at & 1


def local_experts(axis, offset=0):
    z, x, c = position()
    q = lax.broadcasted_iota(jnp.int32, (DESTS, LANES), 0)
    k, flip = q >> 1, q & 1
    core = (c + flip) & 1
    if axis == "x":
        ids = (z << 3) + (((x + k) & 3) << 1) + core
    else:
        ids = (((z + k) & 3) << 3) + (((x + offset) & 3) << 1) + core
    return ids.astype(F32)


def thirds(value):
    high = value.astype(BF16)
    rest = value - high.astype(F32)
    mid = rest.astype(BF16)
    return high, mid, (rest - mid.astype(F32)).astype(BF16)


def stage_body(tokens, cot, ids, weights, tokens_out, cot_out, meta_out):
    tokens_out[...] = tokens[...]
    cot_out[...] = cot[...]
    meta_out[...] = jnp.zeros(meta_out.shape, F32)
    meta_out[0:TOP, :] = ids[...].astype(F32)
    meta_out[8 : 8 + TOP, :] = weights[...]


def stack_body(gate_t, up_t, both_out):
    both_out[0] = gate_t[...]
    both_out[1] = up_t[...]


def selection(meta, experts):
    ids, gate = meta[0:TOP, :], meta[8 : 8 + TOP, :]
    named = jnp.zeros((DESTS, LANES), F32)
    weight = jnp.zeros((DESTS, LANES), F32)
    for j in range(TOP):
        hit = ids[j : j + 1, :] == experts
        named = named + jnp.where(hit, 1.0, 0.0)
        weight = weight + jnp.where(hit, gate[j : j + 1, :], 0.0)
    earlier = lax.broadcasted_iota(jnp.int32, (LANES, LANES), 0) < lax.broadcasted_iota(
        jnp.int32, (LANES, LANES), 1
    )
    before = jnp.dot(
        named.astype(BF16), jnp.where(earlier, 1.0, 0.0).astype(BF16), preferred_element_type=F32
    )
    place = jnp.where(named > 0.5, before, -1.0)
    slot = lax.broadcasted_iota(jnp.int32, (CAP, LANES), 0).astype(F32)
    chosen = jnp.concatenate(
        [
            jnp.where(jnp.broadcast_to(place[q : q + 1, :], (CAP, LANES)) == slot, 1.0, 0.0)
            for q in range(DESTS)
        ],
        axis=0,
    )
    spread = jnp.concatenate(
        [jnp.broadcast_to(weight[q : q + 1, :], (CAP, LANES)) for q in range(DESTS)], axis=0
    )
    return chosen, spread


def dispatch_body(axis, scaled, *refs):
    sources, metas, outs = refs[:4], refs[4:8], refs[8:]
    experts = local_experts(axis)
    for s in range(SIDE):
        chosen, spread = selection(metas[s], experts)
        scale = jnp.sum(chosen * spread, axis=1, keepdims=True) if scaled else None
        chosen = chosen.astype(BF16)

        def column(n, carry, s=s, chosen=chosen, scale=scale):
            at = pl.ds(pl.multiple_of(n * WIDE, WIDE), WIDE)
            rows = jnp.dot(chosen, sources[s][:, at], preferred_element_type=F32)
            if scaled:
                rows = rows * scale
            rows = rows.astype(BF16)
            for q in range(DESTS):
                outs[q][s * CAP : (s + 1) * CAP, at] = rows[q * CAP : (q + 1) * CAP, :]
            return carry

        lax.fori_loop(0, outs[0].shape[1] // WIDE, column, 0)


def contract_rows(left, right):
    return lax.dot_general(left, right, (((0,), (0,)), ((), ())), preferred_element_type=F32)


def contract_lanes(left, right):
    return lax.dot_general(left, right, (((1,), (1,)), ((), ())), preferred_element_type=F32)


def source_rows(blocks, s, columns):
    return jnp.concatenate(
        [blocks[q][s * CAP : (s + 1) * CAP, columns] for q in range(DESTS)], axis=0
    )


def combine_out_body(*refs):
    blocks, metas, outs = refs[:8], refs[8:12], refs[12:]
    experts = local_experts("x")
    for s in range(SIDE):
        chosen, spread = selection(metas[s], experts)
        mix = chosen * spread
        high = mix.astype(BF16)
        mix = jnp.concatenate([high, (mix - high.astype(F32)).astype(BF16)], axis=1)

        def column(n, carry, s=s, mix=mix):
            at = pl.ds(pl.multiple_of(n * TILE, TILE), TILE)
            both = contract_rows(mix, source_rows(blocks, s, at))
            outs[s][:, at] = (both[:LANES, :] + both[LANES:, :]).astype(BF16)
            return carry

        lax.fori_loop(0, outs[0].shape[1] // TILE, column, 0)


def combine_grad_body(*refs):
    blocks, metas, outs = refs[:8], refs[8:12], refs[12:]
    experts = local_experts("z")
    columns = []
    for q in range(DESTS):
        product = blocks[q][ROWS : ROWS + 8, 0 : 3 * LANES].astype(F32)
        product = (product[:, :LANES] + product[:, LANES : 2 * LANES]) + product[:, 2 * LANES :]
        columns.append(jnp.transpose(jnp.broadcast_to(product[0:1, :], (LANES, LANES))))
    for s in range(SIDE):
        chosen, _ = selection(metas[s], experts)
        picked = chosen.astype(BF16)

        def column(n, carry, s=s, picked=picked):
            at = pl.ds(pl.multiple_of(n * TILE, TILE), TILE)
            outs[s][0:LANES, at] = contract_rows(picked, source_rows(blocks, s, at)).astype(BF16)
            return carry

        width = outs[0].shape[1]
        lax.fori_loop(0, width // TILE, column, 0)
        gains = jnp.concatenate(
            [
                jnp.sum(
                    chosen[q * CAP : (q + 1) * CAP, :] * columns[q][s * CAP : (s + 1) * CAP, :],
                    axis=0,
                    keepdims=True,
                )
                for q in range(DESTS)
            ],
            axis=0,
        )
        outs[s][LANES : LANES + 8, 0 : 3 * LANES] = jnp.concatenate(thirds(gains), axis=1)
        outs[s][LANES : LANES + 8, 3 * LANES :] = jnp.zeros((8, width - 3 * LANES), BF16)


def sum_parts_body(*refs):
    parts, out = refs[:4], refs[4]
    out[...] = (
        (parts[0][...].astype(F32) + parts[1][...].astype(F32))
        + (parts[2][...].astype(F32) + parts[3][...].astype(F32))
    ).astype(BF16)


def finish_grad_body(*refs):
    parts, meta, out, gate_out = refs[:4], refs[4], refs[5], refs[6]
    sum_parts_body(*[p.at[0:LANES, :] for p in parts], out)
    ids, gate = meta[0:TOP, :], meta[8 : 8 + TOP, :]
    total = [jnp.zeros((1, LANES), F32) for _ in range(TOP)]
    for k in range(SIDE):
        experts = local_experts("z", k)
        gains = parts[k][LANES : LANES + 8, 0 : 3 * LANES].astype(F32)
        gains = (gains[:, :LANES] + gains[:, LANES : 2 * LANES]) + gains[:, 2 * LANES :]
        for j in range(TOP):
            hit = ids[j : j + 1, :] == experts
            total[j] = total[j] + jnp.sum(jnp.where(hit, gains, 0.0), axis=0, keepdims=True)
    total = [total[j] / gate[j : j + 1, :] for j in range(TOP)]
    gate_out[...] = jnp.concatenate(total, axis=0)


def forward_body(count, *refs):
    blocks, (both, down), outs = refs[:count], refs[count : count + 2], refs[count + 2 : 2 * count + 2]
    gate_factor_out, silu_out, act_out, staged, pre = refs[2 * count + 2 :]
    for i in range(count):
        staged[i * ROWS : (i + 1) * ROWS, :] = blocks[i][...]

    def part(n, carry):
        at = pl.ds(pl.multiple_of(n * 2 * ROWS, 2 * ROWS), 2 * ROWS)

        def project(i, inner):
            pre[i] = contract_lanes(staged[at, :], both[i])
            return inner

        lax.fori_loop(0, 2, project, 0)
        gate_pre, up_pre = pre[0], pre[1]
        sigmoid_val = jax.nn.sigmoid(gate_pre)
        silu_val = gate_pre * sigmoid_val
        factor = up_pre * sigmoid_val * (1.0 + gate_pre * (1.0 - sigmoid_val))
        gate_factor_out[at, :] = factor.astype(BF16)
        silu_out[at, :] = silu_val.astype(BF16)
        act_out[at, :] = (silu_val * up_pre).astype(BF16)
        return carry

    if count == 2:
        part(0, 0)
    else:
        lax.fori_loop(0, count // 2, part, 0)

    def column(n, carry):
        at = pl.ds(pl.multiple_of(n * TILE, TILE), TILE)
        result = jnp.dot(act_out[...], down[:, at], preferred_element_type=F32).astype(BF16)
        for i in range(count):
            outs[i][:, at] = result[i * ROWS : (i + 1) * ROWS, :]
        return carry

    lax.fori_loop(0, down.shape[1] // TILE, column, 0)


def hidden_slices(counts):
    place = {}
    for n, ks in enumerate(counts):
        for i, k in enumerate(ks):
            for flip in range(CORES):
                place[2 * k + flip] = (n, (2 * i + flip) * ROWS)
    return place


def backward_body(kzs, place, arrays, *refs):
    count = 2 * len(kzs)
    cots, refs = refs[:count], refs[count:]
    factors, silus, acts, refs = refs[:arrays], refs[arrays : 2 * arrays], refs[2 * arrays : 3 * arrays], refs[3 * arrays :]
    (both, down), refs = refs[:2], refs[2:]
    outs, gate_grad_out, up_grad_out = refs[:count], refs[count], refs[count + 1]

    def ordered(parts):
        pieces = []
        for kz in kzs:
            for flip in range(CORES):
                for kx in range(SIDE):
                    n, first = place[2 * kx + flip]
                    pieces.append(parts[n][first + kz * CAP : first + (kz + 1) * CAP, :])
        return jnp.concatenate(pieces, axis=0)

    cot = jnp.concatenate([c[...] for c in cots], axis=0)
    act_grad = contract_lanes(cot, down[...])
    gate_grad_out[...] = (act_grad * ordered(factors).astype(F32)).astype(BF16)
    up_grad_out[...] = (act_grad * ordered(silus).astype(F32)).astype(BF16)
    product = jnp.sum(ordered(acts).astype(F32) * act_grad, axis=1, keepdims=True)
    width = down.shape[1]
    for n in range(count):
        part = jnp.broadcast_to(product[n * ROWS : (n + 1) * ROWS, :], (ROWS, LANES))
        part = jnp.transpose(part)[0:8, :]
        outs[n][ROWS : ROWS + 8, 0 : 3 * LANES] = jnp.concatenate(thirds(part), axis=1)
        outs[n][ROWS : ROWS + 8, 3 * LANES :] = jnp.zeros((8, width - 3 * LANES), BF16)

    def column(n, carry):
        at = pl.ds(pl.multiple_of(n * NARROW, NARROW), NARROW)
        result = (
            jnp.dot(gate_grad_out[...], both[0, :, at], preferred_element_type=F32)
            + jnp.dot(up_grad_out[...], both[1, :, at], preferred_element_type=F32)
        ).astype(BF16)
        for i in range(count):
            outs[i][0:ROWS, at] = result[i * ROWS : (i + 1) * ROWS, :]
        return carry

    lax.fori_loop(0, width // NARROW, column, 0)


def in_cot_order(blocks, columns, kzs):
    return jnp.concatenate(
        [
            blocks[2 * kx + flip][kz * CAP : (kz + 1) * CAP, columns]
            for kz in kzs
            for flip in range(CORES)
            for kx in range(SIDE)
        ],
        axis=0,
    )


def column_grad_body(order, arrays, *refs):
    grads, blocks = refs[:arrays], refs[arrays : arrays + 8]
    own, ahead, behind, ahead_kept, behind_kept, turned = refs[arrays + 8 :]
    rep = lax.axis_index("rep")
    hidden, width = own.shape
    half = hidden // 2
    turned[...] = jnp.transpose(jnp.concatenate([h[...] for h in grads], axis=0))
    top, low = slice(0, half), slice(half, hidden)
    places = (
        (own.at[top, :], own.at[low, :]), (ahead_kept, ahead.at[top, :]),
        (ahead.at[low, :], behind.at[low, :]), (behind.at[top, :], behind_kept),
    )

    def chunk(k, carry):
        start = pl.multiple_of(((rep + k) & 3) * width, LANES)
        right = in_cot_order(blocks, pl.ds(start, width), order)
        piece = jnp.dot(turned[...], right, preferred_element_type=F32).astype(BF16)
        for n in range(4):

            @pl.when(k == n)
            def _():
                places[n][0][...] = piece[top, :]
                places[n][1][...] = piece[low, :]

        return carry

    lax.fori_loop(0, 4, chunk, 0)


def row_grad_body(place, arrays, *refs):
    acts, blocks = refs[:arrays], refs[arrays : arrays + 8]
    own, ahead, behind, ahead_kept, behind_kept, turned, whole = refs[arrays + 8 :]
    rep = lax.axis_index("rep")
    height, width = own.shape
    half = width // 2
    pieces = []
    for kz in range(SIDE):
        for flip in range(CORES):
            for kx in range(SIDE):
                n, first = place[2 * kx + flip]
                pieces.append(acts[n][first + kz * CAP : first + (kz + 1) * CAP, :])
    turned[...] = jnp.transpose(jnp.concatenate(pieces, axis=0))

    def column(n, carry):
        at = pl.ds(pl.multiple_of(n * TILE, TILE), TILE)
        right = jnp.concatenate([b[:, at] for b in blocks], axis=0)
        whole[:, at] = jnp.dot(turned[...], right, preferred_element_type=F32).astype(BF16)
        return carry

    lax.fori_loop(0, width // TILE, column, 0)

    def rows_for(k):
        return pl.ds(pl.multiple_of(((rep + k) & 3) * height, 16), height)

    own[...] = whole[rows_for(0), :]
    ahead_kept[...] = whole[rows_for(1), 0:half]
    ahead[:, 0:half] = whole[rows_for(1), half:]
    ahead[:, half:] = whole[rows_for(2), 0:half]
    behind[:, 0:half] = whole[rows_for(3), 0:half]
    behind[:, half:] = whole[rows_for(2), half:]
    behind_kept[...] = whole[rows_for(3), half:]


def relay_body(axis, from_behind, from_ahead, ahead_kept, behind_kept, ahead_out, behind_out):
    far = slice(ahead_kept.shape[axis], None)
    at = (far, slice(None)) if axis == 0 else (slice(None), far)
    ahead_out[...] = (from_behind[at].astype(F32) + ahead_kept[...].astype(F32)).astype(BF16)
    behind_out[...] = (from_ahead[at].astype(F32) + behind_kept[...].astype(F32)).astype(BF16)


def call(body, args, outs, flops, scratch=(), limit=14):
    moved = sum(a.size * a.dtype.itemsize for a in args) + sum(
        o.size * o.dtype.itemsize for o in outs
    )
    vmem = pl.BlockSpec(memory_space=pltpu.VMEM)
    return pl.pallas_call(
        body,
        out_shape=tuple(outs),
        in_specs=[vmem] * len(args),
        out_specs=tuple([vmem] * len(outs)),
        scratch_shapes=list(scratch),
        cost_estimate=pl.CostEstimate(flops=flops, bytes_accessed=moved, transcendentals=0),
        compiler_params=pltpu.CompilerParams(vmem_limit_bytes=limit * 1024 * 1024),
    )(*args)


def per_device(tokens, expert_ids, gate_weights, cotangent, w_gate, w_up, w_down):
    tok_rows, width = tokens.shape
    gate_t = jnp.swapaxes(w_gate[0], 0, 1)
    up_t = jnp.swapaxes(w_up[0], 0, 1)
    down = w_down[0]
    hidden = down.shape[0]

    def block(dtype=BF16, rows=ROWS, columns=width):
        return jax.ShapeDtypeStruct((rows, columns), dtype)

    tall = block(BF16, ROWS + 8)
    own_tokens, own_cot, meta = call(
        stage_body, [tokens, cotangent, expert_ids.T, gate_weights.T],
        [block(), block(), block(F32, 16, tok_rows)], 0, limit=4,
    )
    (both,) = call(
        stack_body, [gate_t, up_t], [jax.ShapeDtypeStruct((2, hidden, width), BF16)], 0,
        limit=14,
    )
    hops = (1, 3, 2)
    token_parts, cot_parts = {0: own_tokens}, {0: own_cot}
    meta_z, meta_x = {0: meta}, {0: meta}
    for k in hops:
        token_parts[k] = move(tokens, "z", k, 0)
        cot_parts[k] = move(cotangent, "x", k, 0)
        meta_z[k] = move(meta, "z", k, 0)
        meta_x[k] = move(meta, "x", k, 0)

    def four(parts):
        return [parts[k] for k in range(SIDE)]

    from_z, from_x = four(token_parts) + four(meta_z), four(cot_parts) + four(meta_x)
    gather_flops = 2 * DESTS * ROWS * LANES * width
    sent = call(
        functools.partial(dispatch_body, "x", False), from_z, [block()] * DESTS, gather_flops,
        limit=10,
    )
    sent_cot = call(
        functools.partial(dispatch_body, "z", True), from_x, [block()] * DESTS, gather_flops,
        limit=10,
    )
    rows = [move(sent[q], "x", q >> 1, q & 1) for q in range(DESTS)]
    cots = [move(sent_cot[q], "z", q >> 1, q & 1) for q in range(DESTS)]

    unit = 2 * ROWS * width * hidden
    groups = ((0, 1, 3), (2,))
    place = hidden_slices(groups)
    out_blocks, gates, ups, acts = {}, [], [], []
    for ks in groups:
        qs = [2 * k + flip for k in ks for flip in range(CORES)]
        count = len(qs)
        results = call(
            functools.partial(forward_body, count),
            [rows[q] for q in qs] + [both, down],
            [block()] * count + [block(BF16, count * ROWS, hidden)] * 3,
            3 * count * unit, [pltpu.VMEM((count * ROWS, width), BF16), pltpu.VMEM((2, 2 * ROWS, hidden), F32)],
            limit=10,
        )
        for q, value in zip(qs, results):
            out_blocks[q] = value
        gates.append(results[count])
        ups.append(results[count + 1])
        acts.append(results[count + 2])
    out_back = [move(out_blocks[q], "x", -(q >> 1), q & 1) for q in range(DESTS)]

    back_groups = ((1, 3), (2, 0))
    row_blocks, gate_grads, up_grads = {}, [], []
    for ks in back_groups:
        qs = [2 * k + flip for k in ks for flip in range(CORES)]
        count = len(qs)
        results = call(
            functools.partial(backward_body, ks, place, len(groups)),
            [cots[q] for q in qs] + gates + ups + acts + [both, down],
            [tall] * count + [block(BF16, count * ROWS, hidden)] * 2,
            3 * count * unit, limit=11,
        )
        for q, value in zip(qs, results):
            row_blocks[q] = value
        gate_grads.append(results[count])
        up_grads.append(results[count + 1])
    rows_back = [move(row_blocks[q], "z", -(q >> 1), q & 1) for q in range(DESTS)]

    order = tuple(k for ks in back_groups for k in ks)

    def chunks(rows_, columns, axis):
        halved = (rows_ // 2, columns) if axis == 0 else (rows_, columns // 2)
        return [block(BF16, rows_, columns)] * 3 + [block(BF16, *halved)] * 2

    down_parts = call(
        functools.partial(row_grad_body, place, len(groups)), acts + cots,
        chunks(hidden // 4, width, 1), 8 * unit,
        [pltpu.VMEM((hidden, DESTS * ROWS), BF16), pltpu.VMEM((hidden, width), BF16)],
    )
    gate_parts, up_parts = [
        call(
            functools.partial(column_grad_body, order, len(back_groups)),
            grads + rows, chunks(hidden, width // 4, 0), 8 * unit,
            [pltpu.VMEM((hidden, DESTS * ROWS), BF16)],
        )
        for grads in (gate_grads, up_grads)
    ]

    def pass_on(value, step):
        return lax.ppermute(value, "rep", [(r, (r + step) % 4) for r in range(4)])

    def reduced(parts, axis):
        own, ahead, behind, ahead_kept, behind_kept = parts
        from_behind = pass_on(ahead, 1)
        from_ahead = pass_on(behind, 3)
        ahead, behind = call(
            functools.partial(relay_body, axis),
            [from_behind, from_ahead, ahead_kept, behind_kept],
            [jax.ShapeDtypeStruct(ahead_kept.shape, BF16)] * 2, ahead_kept.size,
            limit=8,
        )
        relayed_behind = pass_on(ahead, 1)
        relayed_ahead = pass_on(behind, 3)

        def halves(value):
            return [h.astype(F32) for h in jnp.split(value, 2, axis=axis)]

        (own_a, own_b), near_b, near_a = halves(own), halves(from_behind)[0], halves(from_ahead)[0]
        return (
            own_a + near_a + relayed_behind.astype(F32), own_b + near_b + relayed_ahead.astype(F32)
        )

    grad_down = jnp.concatenate(reduced(down_parts, 1), axis=1)[None]
    grad_gate, grad_up = [
        jnp.swapaxes(jnp.concatenate(reduced(parts, 0), axis=0), 0, 1)[None]
        for parts in (gate_parts, up_parts)
    ]

    mixed_parts = call(
        combine_out_body, out_back + from_z[4:], [block()] * SIDE, 2 * gather_flops,
        limit=10,
    )
    mixed_parts = [move(mixed_parts[s], "z", -s, 0) for s in range(SIDE)]
    (mixed,) = call(sum_parts_body, mixed_parts, [block()], 4 * tok_rows * width, limit=4)

    grad_parts = call(
        combine_grad_body, rows_back + from_x[4:], [tall] * SIDE, gather_flops, limit=10,
    )
    grad_parts = [move(grad_parts[s], "x", -s, 0) for s in range(SIDE)]
    token_grad, gate_grad = call(
        finish_grad_body, grad_parts + [meta],
        [block(), block(F32, TOP, LANES)], 4 * tok_rows * width, limit=8,
    )
    return (mixed, token_grad, gate_grad.T, grad_gate, grad_up, grad_down)


def solution(mesh):
    placed = (
        P(("rep", "ep"), None),
        P(("rep", "ep"), None),
        P(("rep", "ep"), None),
        P(("rep", "ep"), None),
        P("ep", None, None),
        P("ep", None, None),
        P("ep", None, None),
    )

    return jax.shard_map(
        per_device,
        mesh=mesh,
        in_specs=placed,
        out_specs=(
            P(("rep", "ep"), None),
            P(("rep", "ep"), None),
            P(("rep", "ep"), None),
            P("ep", "rep", None),
            P("ep", "rep", None),
            P("ep", "rep", None),
        ),
        check_vma=False,
    )
```

```python
import functools

import jax
import jax.numpy as jnp
from jax import lax
from jax.experimental import pallas as pl
from jax.experimental.pallas import tpu as pltpu
from jax.sharding import PartitionSpec as P


F32 = jnp.float32
BF16 = jnp.bfloat16
SIDE = 4
CORES = 2
LANES = 128
CAP = 32
TOP = 6
DESTS = SIDE * CORES
TILE = 512
WIDE = 1024
ROWS = SIDE * CAP


def device_of(z, x, c):
    return (z % SIDE) * SIDE * CORES + (x % SIDE) * CORES + c


def shift_pairs(axis, step, flip):
    pairs = []
    for z in range(SIDE):
        for x in range(SIDE):
            for c in range(CORES):
                there = device_of(z, x + step, c ^ flip) if axis == "x" else device_of(z + step, x, c ^ flip)
                pairs.append((device_of(z, x, c), there))
    return pairs


def move(value, axis, step, flip=0):
    if step % SIDE == 0 and flip == 0:
        return value
    return lax.ppermute(value, "ep", shift_pairs(axis, step, flip))


def position():
    at = lax.axis_index("ep")
    return at >> 3, (at >> 1) & 3, at & 1


def local_experts(axis, offset=0):
    z, x, c = position()
    q = lax.broadcasted_iota(jnp.int32, (DESTS, LANES), 0)
    k, flip = q >> 1, q & 1
    core = (c + flip) & 1
    if axis == "x":
        ids = (z << 3) + (((x + k) & 3) << 1) + core
    else:
        ids = (((z + k) & 3) << 3) + (((x + offset) & 3) << 1) + core
    return ids.astype(F32)


def thirds(value):
    high = value.astype(BF16)
    rest = value - high.astype(F32)
    mid = rest.astype(BF16)
    return high, mid, (rest - mid.astype(F32)).astype(BF16)


def stage_body(tokens, cot, ids, weights, tokens_out, cot_out, meta_out):
    tokens_out[...] = tokens[...]
    cot_out[...] = cot[...]
    meta_out[...] = jnp.zeros(meta_out.shape, F32)
    meta_out[0:TOP, :] = ids[...].astype(F32)
    meta_out[8 : 8 + TOP, :] = weights[...]


def stack_body(gate_t, up_t, both_out):
    both_out[0] = gate_t[...]
    both_out[1] = up_t[...]


def selection(meta, experts):
    ids, gate = meta[0:TOP, :], meta[8 : 8 + TOP, :]
    named = jnp.zeros((DESTS, LANES), F32)
    weight = jnp.zeros((DESTS, LANES), F32)
    for j in range(TOP):
        hit = ids[j : j + 1, :] == experts
        named = named + jnp.where(hit, 1.0, 0.0)
        weight = weight + jnp.where(hit, gate[j : j + 1, :], 0.0)
    earlier = lax.broadcasted_iota(jnp.int32, (LANES, LANES), 0) < lax.broadcasted_iota(
        jnp.int32, (LANES, LANES), 1
    )
    before = jnp.dot(
        named.astype(BF16), jnp.where(earlier, 1.0, 0.0).astype(BF16), preferred_element_type=F32
    )
    place = jnp.where(named > 0.5, before, -1.0)
    slot = lax.broadcasted_iota(jnp.int32, (CAP, LANES), 0).astype(F32)
    chosen = jnp.concatenate(
        [
            jnp.where(jnp.broadcast_to(place[q : q + 1, :], (CAP, LANES)) == slot, 1.0, 0.0)
            for q in range(DESTS)
        ],
        axis=0,
    )
    spread = jnp.concatenate(
        [jnp.broadcast_to(weight[q : q + 1, :], (CAP, LANES)) for q in range(DESTS)], axis=0
    )
    return chosen, spread


def dispatch_body(axis, scaled, *refs):
    sources, metas, outs = refs[:4], refs[4:8], refs[8:]
    experts = local_experts(axis)
    for s in range(SIDE):
        chosen, spread = selection(metas[s], experts)
        scale = jnp.sum(chosen * spread, axis=1, keepdims=True) if scaled else None
        chosen = chosen.astype(BF16)

        def column(n, carry, s=s, chosen=chosen, scale=scale):
            at = pl.ds(pl.multiple_of(n * WIDE, WIDE), WIDE)
            rows = jnp.dot(chosen, sources[s][:, at], preferred_element_type=F32)
            if scaled:
                rows = rows * scale
            rows = rows.astype(BF16)
            for q in range(DESTS):
                outs[q][s * CAP : (s + 1) * CAP, at] = rows[q * CAP : (q + 1) * CAP, :]
            return carry

        lax.fori_loop(0, outs[0].shape[1] // WIDE, column, 0)


def contract_rows(left, right):
    return lax.dot_general(left, right, (((0,), (0,)), ((), ())), preferred_element_type=F32)


def contract_lanes(left, right):
    return lax.dot_general(left, right, (((1,), (1,)), ((), ())), preferred_element_type=F32)


def source_rows(blocks, s, columns):
    return jnp.concatenate(
        [blocks[q][s * CAP : (s + 1) * CAP, columns] for q in range(DESTS)], axis=0
    )


def combine_out_body(*refs):
    blocks, metas, outs = refs[:8], refs[8:12], refs[12:]
    experts = local_experts("x")
    for s in range(SIDE):
        chosen, spread = selection(metas[s], experts)
        mix = chosen * spread
        high = mix.astype(BF16)
        mix = jnp.concatenate([high, (mix - high.astype(F32)).astype(BF16)], axis=1)

        def column(n, carry, s=s, mix=mix):
            at = pl.ds(pl.multiple_of(n * TILE, TILE), TILE)
            both = contract_rows(mix, source_rows(blocks, s, at))
            outs[s][:, at] = (both[:LANES, :] + both[LANES:, :]).astype(BF16)
            return carry

        lax.fori_loop(0, outs[0].shape[1] // TILE, column, 0)


def combine_grad_body(*refs):
    blocks, metas, outs = refs[:8], refs[8:12], refs[12:]
    experts = local_experts("z")
    columns = []
    for q in range(DESTS):
        product = blocks[q][ROWS : ROWS + 8, 0 : 3 * LANES].astype(F32)
        product = (product[:, :LANES] + product[:, LANES : 2 * LANES]) + product[:, 2 * LANES :]
        columns.append(jnp.transpose(jnp.broadcast_to(product[0:1, :], (LANES, LANES))))
    for s in range(SIDE):
        chosen, _ = selection(metas[s], experts)
        picked = chosen.astype(BF16)

        def column(n, carry, s=s, picked=picked):
            at = pl.ds(pl.multiple_of(n * TILE, TILE), TILE)
            outs[s][0:LANES, at] = contract_rows(picked, source_rows(blocks, s, at)).astype(BF16)
            return carry

        width = outs[0].shape[1]
        lax.fori_loop(0, width // TILE, column, 0)
        gains = jnp.concatenate(
            [
                jnp.sum(
                    chosen[q * CAP : (q + 1) * CAP, :] * columns[q][s * CAP : (s + 1) * CAP, :],
                    axis=0,
                    keepdims=True,
                )
                for q in range(DESTS)
            ],
            axis=0,
        )
        outs[s][LANES : LANES + 8, 0 : 3 * LANES] = jnp.concatenate(thirds(gains), axis=1)
        outs[s][LANES : LANES + 8, 3 * LANES :] = jnp.zeros((8, width - 3 * LANES), BF16)


def sum_parts_body(*refs):
    parts, out = refs[:4], refs[4]
    out[...] = (
        (parts[0][...].astype(F32) + parts[1][...].astype(F32))
        + (parts[2][...].astype(F32) + parts[3][...].astype(F32))
    ).astype(BF16)


def finish_grad_body(*refs):
    parts, meta, out, gate_out = refs[:4], refs[4], refs[5], refs[6]
    sum_parts_body(*[p.at[0:LANES, :] for p in parts], out)
    ids, gate = meta[0:TOP, :], meta[8 : 8 + TOP, :]
    total = [jnp.zeros((1, LANES), F32) for _ in range(TOP)]
    for k in range(SIDE):
        experts = local_experts("z", k)
        gains = parts[k][LANES : LANES + 8, 0 : 3 * LANES].astype(F32)
        gains = (gains[:, :LANES] + gains[:, LANES : 2 * LANES]) + gains[:, 2 * LANES :]
        for j in range(TOP):
            hit = ids[j : j + 1, :] == experts
            total[j] = total[j] + jnp.sum(jnp.where(hit, gains, 0.0), axis=0, keepdims=True)
    total = [total[j] / gate[j : j + 1, :] for j in range(TOP)]
    gate_out[...] = jnp.concatenate(total, axis=0)


def forward_body(count, *refs):
    blocks, (both, down), outs = refs[:count], refs[count : count + 2], refs[count + 2 : 2 * count + 2]
    gate_factor_out, silu_out, act_out, staged, pre = refs[2 * count + 2 :]
    for i in range(count):
        staged[i * ROWS : (i + 1) * ROWS, :] = blocks[i][...]

    def part(n, carry):
        at = pl.ds(pl.multiple_of(n * 2 * ROWS, 2 * ROWS), 2 * ROWS)

        def project(i, inner):
            pre[i] = contract_lanes(staged[at, :], both[i])
            return inner

        lax.fori_loop(0, 2, project, 0)
        gate_pre, up_pre = pre[0], pre[1]
        sigmoid_val = jax.nn.sigmoid(gate_pre)
        silu_val = gate_pre * sigmoid_val
        factor = up_pre * sigmoid_val * (1.0 + gate_pre * (1.0 - sigmoid_val))
        gate_factor_out[at, :] = factor.astype(BF16)
        silu_out[at, :] = silu_val.astype(BF16)
        act_out[at, :] = (silu_val * up_pre).astype(BF16)
        return carry

    if count == 2:
        part(0, 0)
    else:
        lax.fori_loop(0, count // 2, part, 0)

    def column(n, carry):
        at = pl.ds(pl.multiple_of(n * TILE, TILE), TILE)
        result = jnp.dot(act_out[...], down[:, at], preferred_element_type=F32).astype(BF16)
        for i in range(count):
            outs[i][:, at] = result[i * ROWS : (i + 1) * ROWS, :]
        return carry

    lax.fori_loop(0, down.shape[1] // TILE, column, 0)


def hidden_slices(counts):
    place = {}
    for n, ks in enumerate(counts):
        for i, k in enumerate(ks):
            for flip in range(CORES):
                place[2 * k + flip] = (n, (2 * i + flip) * ROWS)
    return place


def backward_body(kzs, place, arrays, *refs):
    count = 2 * len(kzs)
    cots, refs = refs[:count], refs[count:]
    factors, silus, acts, refs = refs[:arrays], refs[arrays : 2 * arrays], refs[2 * arrays : 3 * arrays], refs[3 * arrays :]
    (both, down), refs = refs[:2], refs[2:]
    outs, gate_grad_out, up_grad_out = refs[:count], refs[count], refs[count + 1]

    def ordered(parts):
        pieces = []
        for kz in kzs:
            for flip in range(CORES):
                for kx in range(SIDE):
                    n, first = place[2 * kx + flip]
                    pieces.append(parts[n][first + kz * CAP : first + (kz + 1) * CAP, :])
        return jnp.concatenate(pieces, axis=0)

    cot = jnp.concatenate([c[...] for c in cots], axis=0)
    act_grad = contract_lanes(cot, down[...])
    gate_grad_out[...] = (act_grad * ordered(factors).astype(F32)).astype(BF16)
    up_grad_out[...] = (act_grad * ordered(silus).astype(F32)).astype(BF16)
    product = jnp.sum(ordered(acts).astype(F32) * act_grad, axis=1, keepdims=True)
    width = down.shape[1]
    for n in range(count):
        part = jnp.broadcast_to(product[n * ROWS : (n + 1) * ROWS, :], (ROWS, LANES))
        part = jnp.transpose(part)[0:8, :]
        outs[n][ROWS : ROWS + 8, 0 : 3 * LANES] = jnp.concatenate(thirds(part), axis=1)
        outs[n][ROWS : ROWS + 8, 3 * LANES :] = jnp.zeros((8, width - 3 * LANES), BF16)

    def column(n, carry):
        at = pl.ds(pl.multiple_of(n * TILE, TILE), TILE)
        result = (
            jnp.dot(gate_grad_out[...], both[0, :, at], preferred_element_type=F32)
            + jnp.dot(up_grad_out[...], both[1, :, at], preferred_element_type=F32)
        ).astype(BF16)
        for i in range(count):
            outs[i][0:ROWS, at] = result[i * ROWS : (i + 1) * ROWS, :]
        return carry

    lax.fori_loop(0, width // TILE, column, 0)


def in_cot_order(blocks, columns, kzs):
    return jnp.concatenate(
        [
            blocks[2 * kx + flip][kz * CAP : (kz + 1) * CAP, columns]
            for kz in kzs
            for flip in range(CORES)
            for kx in range(SIDE)
        ],
        axis=0,
    )


def column_grad_body(order, arrays, *refs):
    gates, ups, blocks = refs[:arrays], refs[arrays : 2 * arrays], refs[2 * arrays : 2 * arrays + 8]
    own, ahead, behind, ahead_kept, behind_kept, turned, piece = refs[2 * arrays + 8 :]
    rep = lax.axis_index("rep")
    width = own.shape[1]
    hidden = gates[0].shape[1]
    turned[0] = jnp.transpose(jnp.concatenate([h[...] for h in gates], axis=0))
    turned[1] = jnp.transpose(jnp.concatenate([h[...] for h in ups], axis=0))
    places = ((own.at[0:hidden, :], own.at[hidden:, :]), (ahead_kept, ahead.at[0:hidden, :]),
              (ahead.at[hidden:, :], behind.at[hidden:, :]), (behind.at[0:hidden, :], behind_kept))

    def chunk(k, carry):
        start = pl.multiple_of(((rep + k) & 3) * width, LANES)
        right = in_cot_order(blocks, pl.ds(start, width), order)
        for half in range(2):
            piece[half] = jnp.dot(turned[half], right, preferred_element_type=F32).astype(BF16)
        for n in range(4):

            @pl.when(k == n)
            def _():
                for half in range(2):
                    places[n][half][...] = piece[half]

        return carry

    lax.fori_loop(0, 4, chunk, 0)


def row_grad_body(place, arrays, *refs):
    acts, blocks = refs[:arrays], refs[arrays : arrays + 8]
    own, ahead, behind, ahead_kept, behind_kept, turned, whole = refs[arrays + 8 :]
    rep = lax.axis_index("rep")
    height, width = own.shape
    half = width // 2
    pieces = []
    for kz in range(SIDE):
        for flip in range(CORES):
            for kx in range(SIDE):
                n, first = place[2 * kx + flip]
                pieces.append(acts[n][first + kz * CAP : first + (kz + 1) * CAP, :])
    turned[...] = jnp.transpose(jnp.concatenate(pieces, axis=0))

    def column(n, carry):
        at = pl.ds(pl.multiple_of(n * TILE, TILE), TILE)
        right = jnp.concatenate([b[:, at] for b in blocks], axis=0)
        whole[:, at] = jnp.dot(turned[...], right, preferred_element_type=F32).astype(BF16)
        return carry

    lax.fori_loop(0, width // TILE, column, 0)

    def rows_for(k):
        return pl.ds(pl.multiple_of(((rep + k) & 3) * height, 16), height)

    own[...] = whole[rows_for(0), :]
    ahead_kept[...] = whole[rows_for(1), 0:half]
    ahead[:, 0:half] = whole[rows_for(1), half:]
    ahead[:, half:] = whole[rows_for(2), 0:half]
    behind[:, 0:half] = whole[rows_for(3), 0:half]
    behind[:, half:] = whole[rows_for(2), half:]
    behind_kept[...] = whole[rows_for(3), half:]


def relay_body(axis, from_behind, from_ahead, ahead_kept, behind_kept, ahead_out, behind_out):
    far = slice(ahead_kept.shape[axis], None)
    at = (far, slice(None)) if axis == 0 else (slice(None), far)
    ahead_out[...] = (from_behind[at].astype(F32) + ahead_kept[...].astype(F32)).astype(BF16)
    behind_out[...] = (from_ahead[at].astype(F32) + behind_kept[...].astype(F32)).astype(BF16)


def call(body, args, outs, flops, scratch=(), limit=14):
    moved = sum(a.size * a.dtype.itemsize for a in args) + sum(
        o.size * o.dtype.itemsize for o in outs
    )
    vmem = pl.BlockSpec(memory_space=pltpu.VMEM)
    return pl.pallas_call(
        body,
        out_shape=tuple(outs),
        in_specs=[vmem] * len(args),
        out_specs=tuple([vmem] * len(outs)),
        scratch_shapes=list(scratch),
        cost_estimate=pl.CostEstimate(flops=flops, bytes_accessed=moved, transcendentals=0),
        compiler_params=pltpu.CompilerParams(vmem_limit_bytes=limit * 1024 * 1024),
    )(*args)


def per_device(tokens, expert_ids, gate_weights, cotangent, w_gate, w_up, w_down):
    tok_rows, width = tokens.shape
    gate_t = jnp.swapaxes(w_gate[0], 0, 1)
    up_t = jnp.swapaxes(w_up[0], 0, 1)
    down = w_down[0]
    hidden = down.shape[0]

    def block(dtype=BF16, rows=ROWS, columns=width):
        return jax.ShapeDtypeStruct((rows, columns), dtype)

    tall = block(BF16, ROWS + 8)
    own_tokens, own_cot, meta = call(
        stage_body, [tokens, cotangent, expert_ids.T, gate_weights.T],
        [block(), block(), block(F32, 16, tok_rows)], 0, limit=4,
    )
    (both,) = call(
        stack_body, [gate_t, up_t], [jax.ShapeDtypeStruct((2, hidden, width), BF16)], 0,
        limit=14,
    )
    hops = (1, 3, 2)
    token_parts, cot_parts = {0: own_tokens}, {0: own_cot}
    meta_z, meta_x = {0: meta}, {0: meta}
    for k in hops:
        token_parts[k] = move(tokens, "z", k, 0)
        cot_parts[k] = move(cotangent, "x", k, 0)
        meta_z[k] = move(meta, "z", k, 0)
        meta_x[k] = move(meta, "x", k, 0)

    def four(parts):
        return [parts[k] for k in range(SIDE)]

    from_z, from_x = four(token_parts) + four(meta_z), four(cot_parts) + four(meta_x)
    gather_flops = 2 * DESTS * ROWS * LANES * width
    sent = call(
        functools.partial(dispatch_body, "x", False), from_z, [block()] * DESTS, gather_flops,
        limit=10,
    )
    sent_cot = call(
        functools.partial(dispatch_body, "z", True), from_x, [block()] * DESTS, gather_flops,
        limit=10,
    )
    rows = [move(sent[q], "x", q >> 1, q & 1) for q in range(DESTS)]
    cots = [move(sent_cot[q], "z", q >> 1, q & 1) for q in range(DESTS)]

    unit = 2 * ROWS * width * hidden
    groups = ((0, 1), (2, 3))
    place = hidden_slices(groups)
    out_blocks, gates, ups, acts = {}, [], [], []
    for ks in groups:
        qs = [2 * k + flip for k in ks for flip in range(CORES)]
        count = len(qs)
        results = call(
            functools.partial(forward_body, count),
            [rows[q] for q in qs] + [both, down],
            [block()] * count + [block(BF16, count * ROWS, hidden)] * 3,
            3 * count * unit, [pltpu.VMEM((count * ROWS, width), BF16), pltpu.VMEM((2, 2 * ROWS, hidden), F32)],
            limit=10,
        )
        for q, value in zip(qs, results):
            out_blocks[q] = value
        gates.append(results[count])
        ups.append(results[count + 1])
        acts.append(results[count + 2])
    out_back = [move(out_blocks[q], "x", -(q >> 1), q & 1) for q in range(DESTS)]

    back_groups = ((1, 3), (2, 0))
    row_blocks, gate_grads, up_grads = {}, [], []
    for ks in back_groups:
        qs = [2 * k + flip for k in ks for flip in range(CORES)]
        count = len(qs)
        results = call(
            functools.partial(backward_body, ks, place, len(groups)),
            [cots[q] for q in qs] + gates + ups + acts + [both, down],
            [tall] * count + [block(BF16, count * ROWS, hidden)] * 2,
            3 * count * unit, limit=11,
        )
        for q, value in zip(qs, results):
            row_blocks[q] = value
        gate_grads.append(results[count])
        up_grads.append(results[count + 1])
    rows_back = [move(row_blocks[q], "z", -(q >> 1), q & 1) for q in range(DESTS)]

    order = tuple(k for ks in back_groups for k in ks)

    def chunks(rows_, columns, axis):
        halved = (rows_ // 2, columns) if axis == 0 else (rows_, columns // 2)
        return [block(BF16, rows_, columns)] * 3 + [block(BF16, *halved)] * 2

    down_parts = call(
        functools.partial(row_grad_body, place, len(groups)), acts + cots,
        chunks(hidden // 4, width, 1), 8 * unit,
        [pltpu.VMEM((hidden, DESTS * ROWS), BF16), pltpu.VMEM((hidden, width), BF16)],
    )
    both_parts = call(
        functools.partial(column_grad_body, order, len(back_groups)),
        gate_grads + up_grads + rows, chunks(2 * hidden, width // 4, 0), 16 * unit,
        [pltpu.VMEM((2, hidden, DESTS * ROWS), BF16), pltpu.VMEM((2, hidden, width // 4), BF16)],
    )

    def pass_on(value, step):
        return lax.ppermute(value, "rep", [(r, (r + step) % 4) for r in range(4)])

    def reduced(parts, axis):
        own, ahead, behind, ahead_kept, behind_kept = parts
        from_behind = pass_on(ahead, 1)
        from_ahead = pass_on(behind, 3)
        ahead, behind = call(
            functools.partial(relay_body, axis),
            [from_behind, from_ahead, ahead_kept, behind_kept],
            [jax.ShapeDtypeStruct(ahead_kept.shape, BF16)] * 2, ahead_kept.size,
            limit=8,
        )
        relayed_behind = pass_on(ahead, 1)
        relayed_ahead = pass_on(behind, 3)

        def halves(value):
            return [h.astype(F32) for h in jnp.split(value, 2, axis=axis)]

        (own_a, own_b), near_b, near_a = halves(own), halves(from_behind)[0], halves(from_ahead)[0]
        return (
            own_a + near_a + relayed_behind.astype(F32), own_b + near_b + relayed_ahead.astype(F32)
        )

    grad_down = jnp.concatenate(reduced(down_parts, 1), axis=1)[None]
    grad_gate, grad_up = [jnp.swapaxes(g, 0, 1)[None] for g in reduced(both_parts, 0)]

    mixed_parts = call(
        combine_out_body, out_back + from_z[4:], [block()] * SIDE, 2 * gather_flops,
        limit=10,
    )
    mixed_parts = [move(mixed_parts[s], "z", -s, 0) for s in range(SIDE)]
    (mixed,) = call(sum_parts_body, mixed_parts, [block()], 4 * tok_rows * width, limit=4)

    grad_parts = call(
        combine_grad_body, rows_back + from_x[4:], [tall] * SIDE, gather_flops, limit=10,
    )
    grad_parts = [move(grad_parts[s], "x", -s, 0) for s in range(SIDE)]
    token_grad, gate_grad = call(
        finish_grad_body, grad_parts + [meta],
        [block(), block(F32, TOP, LANES)], 4 * tok_rows * width, limit=8,
    )
    return (mixed, token_grad, gate_grad.T, grad_gate, grad_up, grad_down)


def solution(mesh):
    placed = (
        P(("rep", "ep"), None),
        P(("rep", "ep"), None),
        P(("rep", "ep"), None),
        P(("rep", "ep"), None),
        P("ep", None, None),
        P("ep", None, None),
        P("ep", None, None),
    )

    return jax.shard_map(
        per_device,
        mesh=mesh,
        in_specs=placed,
        out_specs=(
            P(("rep", "ep"), None),
            P(("rep", "ep"), None),
            P(("rep", "ep"), None),
            P("ep", "rep", None),
            P("ep", "rep", None),
            P("ep", "rep", None),
        ),
        check_vma=False,
    )
```

```python
import functools

import jax
import jax.numpy as jnp
from jax import lax
from jax.experimental import pallas as pl
from jax.experimental.pallas import tpu as pltpu
from jax.sharding import PartitionSpec as P


F32 = jnp.float32
BF16 = jnp.bfloat16
SIDE = 4
CORES = 2
LANES = 128
CAP = 32
TOP = 6
DESTS = SIDE * CORES
TILE = 512
WIDE = 1024
ROWS = SIDE * CAP


def device_of(z, x, c):
    return (z % SIDE) * SIDE * CORES + (x % SIDE) * CORES + c


def shift_pairs(axis, step, flip):
    pairs = []
    for z in range(SIDE):
        for x in range(SIDE):
            for c in range(CORES):
                there = device_of(z, x + step, c ^ flip) if axis == "x" else device_of(z + step, x, c ^ flip)
                pairs.append((device_of(z, x, c), there))
    return pairs


def move(value, axis, step, flip=0):
    if step % SIDE == 0 and flip == 0:
        return value
    return lax.ppermute(value, "ep", shift_pairs(axis, step, flip))


def position():
    at = lax.axis_index("ep")
    return at >> 3, (at >> 1) & 3, at & 1


def local_experts(axis, offset=0):
    z, x, c = position()
    q = lax.broadcasted_iota(jnp.int32, (DESTS, LANES), 0)
    k, flip = q >> 1, q & 1
    core = (c + flip) & 1
    if axis == "x":
        ids = (z << 3) + (((x + k) & 3) << 1) + core
    else:
        ids = (((z + k) & 3) << 3) + (((x + offset) & 3) << 1) + core
    return ids.astype(F32)


def thirds(value):
    high = value.astype(BF16)
    rest = value - high.astype(F32)
    mid = rest.astype(BF16)
    return high, mid, (rest - mid.astype(F32)).astype(BF16)


def stage_body(tokens, cot, ids, weights, tokens_out, cot_out, meta_out):
    tokens_out[...] = tokens[...]
    cot_out[...] = cot[...]
    meta_out[...] = jnp.zeros(meta_out.shape, F32)
    meta_out[0:TOP, :] = ids[...].astype(F32)
    meta_out[8 : 8 + TOP, :] = weights[...]


def stack_body(gate_t, up_t, both_out):
    both_out[0] = gate_t[...]
    both_out[1] = up_t[...]


def selection(meta, experts):
    ids, gate = meta[0:TOP, :], meta[8 : 8 + TOP, :]
    named = jnp.zeros((DESTS, LANES), F32)
    weight = jnp.zeros((DESTS, LANES), F32)
    for j in range(TOP):
        hit = ids[j : j + 1, :] == experts
        named = named + jnp.where(hit, 1.0, 0.0)
        weight = weight + jnp.where(hit, gate[j : j + 1, :], 0.0)
    earlier = lax.broadcasted_iota(jnp.int32, (LANES, LANES), 0) < lax.broadcasted_iota(
        jnp.int32, (LANES, LANES), 1
    )
    before = jnp.dot(
        named.astype(BF16), jnp.where(earlier, 1.0, 0.0).astype(BF16), preferred_element_type=F32
    )
    place = jnp.where(named > 0.5, before, -1.0)
    slot = lax.broadcasted_iota(jnp.int32, (CAP, LANES), 0).astype(F32)
    chosen = jnp.concatenate(
        [
            jnp.where(jnp.broadcast_to(place[q : q + 1, :], (CAP, LANES)) == slot, 1.0, 0.0)
            for q in range(DESTS)
        ],
        axis=0,
    )
    spread = jnp.concatenate(
        [jnp.broadcast_to(weight[q : q + 1, :], (CAP, LANES)) for q in range(DESTS)], axis=0
    )
    return chosen, spread


def dispatch_body(axis, scaled, *refs):
    sources, metas, outs = refs[:4], refs[4:8], refs[8:]
    experts = local_experts(axis)
    for s in range(SIDE):
        chosen, spread = selection(metas[s], experts)
        scale = jnp.sum(chosen * spread, axis=1, keepdims=True) if scaled else None
        chosen = chosen.astype(BF16)

        def column(n, carry, s=s, chosen=chosen, scale=scale):
            at = pl.ds(pl.multiple_of(n * WIDE, WIDE), WIDE)
            rows = jnp.dot(chosen, sources[s][:, at], preferred_element_type=F32)
            if scaled:
                rows = rows * scale
            rows = rows.astype(BF16)
            for q in range(DESTS):
                outs[q][s * CAP : (s + 1) * CAP, at] = rows[q * CAP : (q + 1) * CAP, :]
            return carry

        lax.fori_loop(0, outs[0].shape[1] // WIDE, column, 0)


def contract_rows(left, right):
    return lax.dot_general(left, right, (((0,), (0,)), ((), ())), preferred_element_type=F32)


def contract_lanes(left, right):
    return lax.dot_general(left, right, (((1,), (1,)), ((), ())), preferred_element_type=F32)


def source_rows(blocks, s, columns):
    return jnp.concatenate(
        [blocks[q][s * CAP : (s + 1) * CAP, columns] for q in range(DESTS)], axis=0
    )


def combine_out_body(*refs):
    blocks, metas, outs = refs[:8], refs[8:12], refs[12:]
    experts = local_experts("x")
    for s in range(SIDE):
        chosen, spread = selection(metas[s], experts)
        mix = chosen * spread
        high = mix.astype(BF16)
        mix = jnp.concatenate([high, (mix - high.astype(F32)).astype(BF16)], axis=1)

        def column(n, carry, s=s, mix=mix):
            at = pl.ds(pl.multiple_of(n * TILE, TILE), TILE)
            both = contract_rows(mix, source_rows(blocks, s, at))
            outs[s][:, at] = (both[:LANES, :] + both[LANES:, :]).astype(BF16)
            return carry

        lax.fori_loop(0, outs[0].shape[1] // TILE, column, 0)


def combine_grad_body(*refs):
    blocks, metas, outs = refs[:8], refs[8:12], refs[12:]
    experts = local_experts("z")
    columns = []
    for q in range(DESTS):
        product = blocks[q][ROWS : ROWS + 8, 0 : 3 * LANES].astype(F32)
        product = (product[:, :LANES] + product[:, LANES : 2 * LANES]) + product[:, 2 * LANES :]
        columns.append(jnp.transpose(jnp.broadcast_to(product[0:1, :], (LANES, LANES))))
    for s in range(SIDE):
        chosen, _ = selection(metas[s], experts)
        picked = chosen.astype(BF16)

        def column(n, carry, s=s, picked=picked):
            at = pl.ds(pl.multiple_of(n * TILE, TILE), TILE)
            outs[s][0:LANES, at] = contract_rows(picked, source_rows(blocks, s, at)).astype(BF16)
            return carry

        width = outs[0].shape[1]
        lax.fori_loop(0, width // TILE, column, 0)
        gains = jnp.concatenate(
            [
                jnp.sum(
                    chosen[q * CAP : (q + 1) * CAP, :] * columns[q][s * CAP : (s + 1) * CAP, :],
                    axis=0,
                    keepdims=True,
                )
                for q in range(DESTS)
            ],
            axis=0,
        )
        outs[s][LANES : LANES + 8, 0 : 3 * LANES] = jnp.concatenate(thirds(gains), axis=1)
        outs[s][LANES : LANES + 8, 3 * LANES :] = jnp.zeros((8, width - 3 * LANES), BF16)


def sum_parts_body(*refs):
    parts, out = refs[:4], refs[4]
    out[...] = (
        (parts[0][...].astype(F32) + parts[1][...].astype(F32))
        + (parts[2][...].astype(F32) + parts[3][...].astype(F32))
    ).astype(BF16)


def finish_grad_body(*refs):
    parts, meta, out, gate_out = refs[:4], refs[4], refs[5], refs[6]
    sum_parts_body(*[p.at[0:LANES, :] for p in parts], out)
    ids, gate = meta[0:TOP, :], meta[8 : 8 + TOP, :]
    total = [jnp.zeros((1, LANES), F32) for _ in range(TOP)]
    for k in range(SIDE):
        experts = local_experts("z", k)
        gains = parts[k][LANES : LANES + 8, 0 : 3 * LANES].astype(F32)
        gains = (gains[:, :LANES] + gains[:, LANES : 2 * LANES]) + gains[:, 2 * LANES :]
        for j in range(TOP):
            hit = ids[j : j + 1, :] == experts
            total[j] = total[j] + jnp.sum(jnp.where(hit, gains, 0.0), axis=0, keepdims=True)
    total = [total[j] / gate[j : j + 1, :] for j in range(TOP)]
    gate_out[...] = jnp.concatenate(total, axis=0)


def forward_body(count, *refs):
    blocks, (both, down), outs = refs[:count], refs[count : count + 2], refs[count + 2 : 2 * count + 2]
    gate_factor_out, silu_out, act_out, staged, pre = refs[2 * count + 2 :]
    for i in range(count):
        staged[i * ROWS : (i + 1) * ROWS, :] = blocks[i][...]

    def part(n, carry):
        at = pl.ds(pl.multiple_of(n * 2 * ROWS, 2 * ROWS), 2 * ROWS)

        def project(i, inner):
            pre[i] = contract_lanes(staged[at, :], both[i])
            return inner

        lax.fori_loop(0, 2, project, 0)
        gate_pre, up_pre = pre[0], pre[1]
        sigmoid_val = jax.nn.sigmoid(gate_pre)
        silu_val = gate_pre * sigmoid_val
        factor = up_pre * sigmoid_val * (1.0 + gate_pre * (1.0 - sigmoid_val))
        gate_factor_out[at, :] = factor.astype(BF16)
        silu_out[at, :] = silu_val.astype(BF16)
        act_out[at, :] = (silu_val * up_pre).astype(BF16)
        return carry

    if count == 2:
        part(0, 0)
    else:
        lax.fori_loop(0, count // 2, part, 0)

    def column(n, carry):
        at = pl.ds(pl.multiple_of(n * TILE, TILE), TILE)
        result = jnp.dot(act_out[...], down[:, at], preferred_element_type=F32).astype(BF16)
        for i in range(count):
            outs[i][:, at] = result[i * ROWS : (i + 1) * ROWS, :]
        return carry

    lax.fori_loop(0, down.shape[1] // TILE, column, 0)


def hidden_slices(counts):
    place = {}
    for n, ks in enumerate(counts):
        for i, k in enumerate(ks):
            for flip in range(CORES):
                place[2 * k + flip] = (n, (2 * i + flip) * ROWS)
    return place


def backward_body(kzs, place, arrays, *refs):
    count = 2 * len(kzs)
    cots, refs = refs[:count], refs[count:]
    factors, silus, acts, refs = refs[:arrays], refs[arrays : 2 * arrays], refs[2 * arrays : 3 * arrays], refs[3 * arrays :]
    (both, down), refs = refs[:2], refs[2:]
    outs, gate_grad_out, up_grad_out = refs[:count], refs[count], refs[count + 1]

    def ordered(parts):
        pieces = []
        for kz in kzs:
            for flip in range(CORES):
                for kx in range(SIDE):
                    n, first = place[2 * kx + flip]
                    pieces.append(parts[n][first + kz * CAP : first + (kz + 1) * CAP, :])
        return jnp.concatenate(pieces, axis=0)

    cot = jnp.concatenate([c[...] for c in cots], axis=0)
    act_grad = contract_lanes(cot, down[...])
    gate_grad_out[...] = (act_grad * ordered(factors).astype(F32)).astype(BF16)
    up_grad_out[...] = (act_grad * ordered(silus).astype(F32)).astype(BF16)
    product = jnp.sum(ordered(acts).astype(F32) * act_grad, axis=1, keepdims=True)
    width = down.shape[1]
    for n in range(count):
        part = jnp.broadcast_to(product[n * ROWS : (n + 1) * ROWS, :], (ROWS, LANES))
        part = jnp.transpose(part)[0:8, :]
        outs[n][ROWS : ROWS + 8, 0 : 3 * LANES] = jnp.concatenate(thirds(part), axis=1)
        outs[n][ROWS : ROWS + 8, 3 * LANES :] = jnp.zeros((8, width - 3 * LANES), BF16)

    def column(n, carry):
        at = pl.ds(pl.multiple_of(n * TILE, TILE), TILE)
        result = (
            jnp.dot(gate_grad_out[...], both[0, :, at], preferred_element_type=F32)
            + jnp.dot(up_grad_out[...], both[1, :, at], preferred_element_type=F32)
        ).astype(BF16)
        for i in range(count):
            outs[i][0:ROWS, at] = result[i * ROWS : (i + 1) * ROWS, :]
        return carry

    lax.fori_loop(0, width // TILE, column, 0)


def in_cot_order(blocks, columns, kzs):
    return jnp.concatenate(
        [
            blocks[2 * kx + flip][kz * CAP : (kz + 1) * CAP, columns]
            for kz in kzs
            for flip in range(CORES)
            for kx in range(SIDE)
        ],
        axis=0,
    )


def column_grad_body(order, arrays, *refs):
    gates, ups, blocks = refs[:arrays], refs[arrays : 2 * arrays], refs[2 * arrays : 2 * arrays + 8]
    own, ahead, behind, ahead_kept, behind_kept, turned, piece, columns = refs[2 * arrays + 8 :]
    rep = lax.axis_index("rep")
    width = own.shape[1]
    hidden = gates[0].shape[1]
    turned[0] = jnp.transpose(jnp.concatenate([h[...] for h in gates], axis=0))
    turned[1] = jnp.transpose(jnp.concatenate([h[...] for h in ups], axis=0))
    places = ((own.at[0:hidden, :], own.at[hidden:, :]), (ahead_kept, ahead.at[0:hidden, :]),
              (ahead.at[hidden:, :], behind.at[hidden:, :]), (behind.at[0:hidden, :], behind_kept))

    def chunk(k, carry):
        start = pl.multiple_of(((rep + k) & 3) * width, LANES)
        columns[...] = in_cot_order(blocks, pl.ds(start, width), order)

        def product(half, inner):
            piece[half] = jnp.dot(turned[half], columns[...], preferred_element_type=F32).astype(BF16)
            return inner

        lax.fori_loop(0, 2, product, 0)
        for n in range(4):

            @pl.when(k == n)
            def _():
                for half in range(2):
                    places[n][half][...] = piece[half]

        return carry

    lax.fori_loop(0, 4, chunk, 0)


def row_grad_body(place, arrays, *refs):
    acts, blocks = refs[:arrays], refs[arrays : arrays + 8]
    own, ahead, behind, ahead_kept, behind_kept, turned, whole = refs[arrays + 8 :]
    rep = lax.axis_index("rep")
    height, width = own.shape
    half = width // 2
    pieces = []
    for kz in range(SIDE):
        for flip in range(CORES):
            for kx in range(SIDE):
                n, first = place[2 * kx + flip]
                pieces.append(acts[n][first + kz * CAP : first + (kz + 1) * CAP, :])
    turned[...] = jnp.transpose(jnp.concatenate(pieces, axis=0))

    def column(n, carry):
        at = pl.ds(pl.multiple_of(n * TILE, TILE), TILE)
        right = jnp.concatenate([b[:, at] for b in blocks], axis=0)
        whole[:, at] = jnp.dot(turned[...], right, preferred_element_type=F32).astype(BF16)
        return carry

    lax.fori_loop(0, width // TILE, column, 0)

    def rows_for(k):
        return pl.ds(pl.multiple_of(((rep + k) & 3) * height, 16), height)

    own[...] = whole[rows_for(0), :]
    ahead_kept[...] = whole[rows_for(1), 0:half]
    ahead[:, 0:half] = whole[rows_for(1), half:]
    ahead[:, half:] = whole[rows_for(2), 0:half]
    behind[:, 0:half] = whole[rows_for(3), 0:half]
    behind[:, half:] = whole[rows_for(2), half:]
    behind_kept[...] = whole[rows_for(3), half:]


def relay_body(axis, from_behind, from_ahead, ahead_kept, behind_kept, ahead_out, behind_out):
    far = slice(ahead_kept.shape[axis], None)
    at = (far, slice(None)) if axis == 0 else (slice(None), far)
    ahead_out[...] = (from_behind[at].astype(F32) + ahead_kept[...].astype(F32)).astype(BF16)
    behind_out[...] = (from_ahead[at].astype(F32) + behind_kept[...].astype(F32)).astype(BF16)


def call(body, args, outs, flops, scratch=(), limit=14):
    moved = sum(a.size * a.dtype.itemsize for a in args) + sum(
        o.size * o.dtype.itemsize for o in outs
    )
    vmem = pl.BlockSpec(memory_space=pltpu.VMEM)
    return pl.pallas_call(
        body,
        out_shape=tuple(outs),
        in_specs=[vmem] * len(args),
        out_specs=tuple([vmem] * len(outs)),
        scratch_shapes=list(scratch),
        cost_estimate=pl.CostEstimate(flops=flops, bytes_accessed=moved, transcendentals=0),
        compiler_params=pltpu.CompilerParams(vmem_limit_bytes=limit * 1024 * 1024),
    )(*args)


def per_device(tokens, expert_ids, gate_weights, cotangent, w_gate, w_up, w_down):
    tok_rows, width = tokens.shape
    gate_t = jnp.swapaxes(w_gate[0], 0, 1)
    up_t = jnp.swapaxes(w_up[0], 0, 1)
    down = w_down[0]
    hidden = down.shape[0]

    def block(dtype=BF16, rows=ROWS, columns=width):
        return jax.ShapeDtypeStruct((rows, columns), dtype)

    tall = block(BF16, ROWS + 8)
    own_tokens, own_cot, meta = call(
        stage_body, [tokens, cotangent, expert_ids.T, gate_weights.T],
        [block(), block(), block(F32, 16, tok_rows)], 0, limit=4,
    )
    (both,) = call(
        stack_body, [gate_t, up_t], [jax.ShapeDtypeStruct((2, hidden, width), BF16)], 0,
        limit=14,
    )
    hops = (1, 3, 2)
    token_parts, cot_parts = {0: own_tokens}, {0: own_cot}
    meta_z, meta_x = {0: meta}, {0: meta}
    for k in hops:
        token_parts[k] = move(tokens, "z", k, 0)
        cot_parts[k] = move(cotangent, "x", k, 0)
        meta_z[k] = move(meta, "z", k, 0)
        meta_x[k] = move(meta, "x", k, 0)

    def four(parts):
        return [parts[k] for k in range(SIDE)]

    from_z, from_x = four(token_parts) + four(meta_z), four(cot_parts) + four(meta_x)
    gather_flops = 2 * DESTS * ROWS * LANES * width
    sent = call(
        functools.partial(dispatch_body, "x", False), from_z, [block()] * DESTS, gather_flops,
        limit=10,
    )
    sent_cot = call(
        functools.partial(dispatch_body, "z", True), from_x, [block()] * DESTS, gather_flops,
        limit=10,
    )
    rows = [move(sent[q], "x", q >> 1, q & 1) for q in range(DESTS)]
    cots = [move(sent_cot[q], "z", q >> 1, q & 1) for q in range(DESTS)]

    unit = 2 * ROWS * width * hidden
    groups = ((0,), (1, 3), (2,))
    place = hidden_slices(groups)
    out_blocks, gates, ups, acts = {}, [], [], []
    for ks in groups:
        qs = [2 * k + flip for k in ks for flip in range(CORES)]
        count = len(qs)
        results = call(
            functools.partial(forward_body, count),
            [rows[q] for q in qs] + [both, down],
            [block()] * count + [block(BF16, count * ROWS, hidden)] * 3,
            3 * count * unit, [pltpu.VMEM((count * ROWS, width), BF16), pltpu.VMEM((2, 2 * ROWS, hidden), F32)],
            limit=10,
        )
        for q, value in zip(qs, results):
            out_blocks[q] = value
        gates.append(results[count])
        ups.append(results[count + 1])
        acts.append(results[count + 2])
    out_back = [move(out_blocks[q], "x", -(q >> 1), q & 1) for q in range(DESTS)]

    back_groups = ((1, 3), (2, 0))
    row_blocks, gate_grads, up_grads = {}, [], []
    for ks in back_groups:
        qs = [2 * k + flip for k in ks for flip in range(CORES)]
        count = len(qs)
        results = call(
            functools.partial(backward_body, ks, place, len(groups)),
            [cots[q] for q in qs] + gates + ups + acts + [both, down],
            [tall] * count + [block(BF16, count * ROWS, hidden)] * 2,
            3 * count * unit, limit=11,
        )
        for q, value in zip(qs, results):
            row_blocks[q] = value
        gate_grads.append(results[count])
        up_grads.append(results[count + 1])
    rows_back = [move(row_blocks[q], "z", -(q >> 1), q & 1) for q in range(DESTS)]

    order = tuple(k for ks in back_groups for k in ks)

    def chunks(rows_, columns, axis):
        halved = (rows_ // 2, columns) if axis == 0 else (rows_, columns // 2)
        return [block(BF16, rows_, columns)] * 3 + [block(BF16, *halved)] * 2

    down_parts = call(
        functools.partial(row_grad_body, place, len(groups)), acts + cots,
        chunks(hidden // 4, width, 1), 8 * unit,
        [pltpu.VMEM((hidden, DESTS * ROWS), BF16), pltpu.VMEM((hidden, width), BF16)],
    )
    both_parts = call(
        functools.partial(column_grad_body, order, len(back_groups)),
        gate_grads + up_grads + rows, chunks(2 * hidden, width // 4, 0), 16 * unit,
        [pltpu.VMEM((2, hidden, DESTS * ROWS), BF16), pltpu.VMEM((2, hidden, width // 4), BF16),
         pltpu.VMEM((DESTS * ROWS, width // 4), BF16)],
    )

    def pass_on(value, step):
        return lax.ppermute(value, "rep", [(r, (r + step) % 4) for r in range(4)])

    def reduced(parts, axis):
        own, ahead, behind, ahead_kept, behind_kept = parts
        from_behind = pass_on(ahead, 1)
        from_ahead = pass_on(behind, 3)
        ahead, behind = call(
            functools.partial(relay_body, axis),
            [from_behind, from_ahead, ahead_kept, behind_kept],
            [jax.ShapeDtypeStruct(ahead_kept.shape, BF16)] * 2, ahead_kept.size,
            limit=8,
        )
        relayed_behind = pass_on(ahead, 1)
        relayed_ahead = pass_on(behind, 3)

        def halves(value):
            return [h.astype(F32) for h in jnp.split(value, 2, axis=axis)]

        (own_a, own_b), near_b, near_a = halves(own), halves(from_behind)[0], halves(from_ahead)[0]
        return (
            own_a + near_a + relayed_behind.astype(F32), own_b + near_b + relayed_ahead.astype(F32)
        )

    grad_down = jnp.concatenate(reduced(down_parts, 1), axis=1)[None]
    grad_gate, grad_up = [jnp.swapaxes(g, 0, 1)[None] for g in reduced(both_parts, 0)]

    mixed_parts = call(
        combine_out_body, out_back + from_z[4:], [block()] * SIDE, 2 * gather_flops,
        limit=10,
    )
    mixed_parts = [move(mixed_parts[s], "z", -s, 0) for s in range(SIDE)]
    (mixed,) = call(sum_parts_body, mixed_parts, [block()], 4 * tok_rows * width, limit=4)

    grad_parts = call(
        combine_grad_body, rows_back + from_x[4:], [tall] * SIDE, gather_flops, limit=10,
    )
    grad_parts = [move(grad_parts[s], "x", -s, 0) for s in range(SIDE)]
    token_grad, gate_grad = call(
        finish_grad_body, grad_parts + [meta],
        [block(), block(F32, TOP, LANES)], 4 * tok_rows * width, limit=8,
    )
    return (mixed, token_grad, gate_grad.T, grad_gate, grad_up, grad_down)


def solution(mesh):
    placed = (
        P(("rep", "ep"), None),
        P(("rep", "ep"), None),
        P(("rep", "ep"), None),
        P(("rep", "ep"), None),
        P("ep", None, None),
        P("ep", None, None),
        P("ep", None, None),
    )

    return jax.shard_map(
        per_device,
        mesh=mesh,
        in_specs=placed,
        out_specs=(
            P(("rep", "ep"), None),
            P(("rep", "ep"), None),
            P(("rep", "ep"), None),
            P("ep", "rep", None),
            P("ep", "rep", None),
            P("ep", "rep", None),
        ),
        check_vma=False,
    )
```
